256 devices in a mesh: ckpt: 16 (over z, core), rows: 16 (over y, x).
Axes of the slice: x: 4, y: 4, z: 8, core: 2. Of those that a mesh axis runs over, the one named last changes fastest.
Arguments:
- deltas: bfloat16 [16, 4096, 14336], P('ckpt', 'rows'), may hold values from -24 to 24
- start_basis: bfloat16 [16, 14336, 64], P('ckpt', 'rows'), may hold values from -6 to 6
- edit_order: int32 [16], replicated, may hold values from 0 to 15, each once
Outputs:
- merged: bfloat16 [4096, 14336], P('rows', 'ckpt')
The draws below stay inside these ranges and needn't reach their ends.
Inputs may be any that keep to these rules, and one draw needn't show every extreme that they name: `edit_order`: a permutation: each of 0 to 15 appears once.
All inputs are finite; a program needn't handle non-finite values.
Results may differ from the reference program's by a relative error of at most 0.034.
Values may be sent and summed in bfloat16 or wider, within the bound.
A program may use at most 64 MiB of HBM per device.

```python
import math
import jax
import jax.numpy as jnp
from jax import lax

D = 4096
FF = 14336
RANK = 64
SUB_ITERS = 2
NS_ITERS = 4
CKPT = 16
N_ROWS = 16


def unit_field(key, shape):
    return jax.random.normal(key, shape, jnp.float32)


def draw_deltas(key, part):
    common = unit_field(jax.random.fold_in(key, 11), (D, FF))
    pairing = jax.random.permutation(jax.random.fold_in(key, 12), N_ROWS)
    row_block = jnp.arange(D) // (D // N_ROWS)
    col_block = jnp.arange(FF) // (FF // N_ROWS)
    spike_factor = jnp.where(pairing[row_block][:, None] == col_block[None, :], 2.0, 1.0).astype(jnp.float32)
    factor = 2.0 * spike_factor

    def draw_single(ckpt_index):
        private = unit_field(jax.random.fold_in(key, 100 + ckpt_index), (D, FF))
        combined = factor * (math.sqrt(0.9) * common + math.sqrt(0.1) * private)
        return jnp.clip(combined, -24.0, 24.0).astype(jnp.bfloat16)
    return lax.map(draw_single, jnp.arange(CKPT))


def draw_start_basis(key, part):
    common = unit_field(jax.random.fold_in(key, 21), (FF, RANK))
    private = unit_field(jax.random.fold_in(key, 22), (CKPT, FF, RANK))
    combined = math.sqrt(0.9) * common[None, :, :] + math.sqrt(0.1) * private
    return jnp.clip(combined, -6.0, 6.0).astype(jnp.bfloat16)


def setup_inputs(seed: int = 0) -> dict:
    key_of = jax.random.split(jax.random.key(seed), 4)
    return {
        "deltas": draw_deltas(jax.random.fold_in(key_of[3], 71), 0),
        "start_basis": draw_start_basis(jax.random.fold_in(key_of[3], 71), 0),
        "edit_order": jax.random.permutation(key_of[2], CKPT).astype(jnp.int32),
    }


def orthonormal(raw):
    gram_matrix = jnp.dot(raw.T, raw, precision=lax.Precision.HIGHEST)
    lower_factor = jnp.linalg.cholesky(gram_matrix)
    basis_new = lax.linalg.triangular_solve(lower_factor, raw, left_side=False, lower=True, transpose_a=True)
    return (basis_new.astype(jnp.bfloat16), lower_factor)

def subspace(pair):
    changes, start = pair
    basis_now = start
    left_basis = jnp.zeros((D, RANK), jnp.bfloat16)
    lower_factor = jnp.zeros((RANK, RANK), jnp.float32)
    for sweep in range(SUB_ITERS):
        left_raw = jnp.dot(changes.astype(jnp.float32), basis_now.astype(jnp.float32), preferred_element_type=jnp.float32)
        left_basis, unused = orthonormal(left_raw)
        right_raw = lax.dot_general(changes.astype(jnp.float32), left_basis.astype(jnp.float32), (((0,), (0,)), ((), ())), preferred_element_type=jnp.float32)
        basis_now, lower_factor = orthonormal(right_raw)
    return (left_basis, basis_now, lower_factor)

def whiten(stacked):
    current = stacked
    for step in range(NS_ITERS):
        gram_matrix = jnp.dot(current.T.astype(jnp.float32), current.astype(jnp.float32), preferred_element_type=jnp.float32)
        if step == 0:
            lead_factor = 1.5 / math.sqrt(CKPT)
            tail_factor = -0.5 / (CKPT * math.sqrt(CKPT))
        else:
            lead_factor = 1.5
            tail_factor = -0.5
        product = jnp.dot(current.astype(jnp.float32), gram_matrix, precision=lax.Precision.HIGHEST)
        current = (lead_factor * current.astype(jnp.float32) + tail_factor * product).astype(jnp.bfloat16)
    return current

def reference(deltas, start_basis, edit_order):
    lefts, rights, lowers = lax.map(subspace, (deltas, start_basis))
    left_stack = lefts.transpose(1, 0, 2).reshape(D, CKPT * RANK)
    right_stack = rights.transpose(1, 0, 2).reshape(FF, CKPT * RANK)
    left_white = whiten(left_stack)
    right_white = whiten(right_stack)
    weights = (1 + edit_order).astype(jnp.float32) / CKPT
    middles = lowers * weights[:, None, None]
    left_blocks = left_white.reshape(D, CKPT, RANK).astype(jnp.float32)
    scaled_left = jnp.einsum('dcr,crs->dcs', left_blocks, middles, precision=lax.Precision.HIGHEST)
    scaled_left = scaled_left.astype(jnp.bfloat16).reshape(D, CKPT * RANK)
    merged = lax.dot_general(scaled_left.astype(jnp.float32), right_white.astype(jnp.float32), (((1,), (1,)), ((), ())), preferred_element_type=jnp.float32)
    return merged.astype(jnp.bfloat16)
```

```python
import jax
import jax.numpy as jnp
from jax import lax
from jax.experimental import pallas as pl
from jax.experimental.pallas import tpu as pltpu
from jax.sharding import PartitionSpec as P

RANK = 64
NS_ITERS = 4
N = 16
COLS = 896
BF = jnp.bfloat16
F32 = jnp.float32
MESH = pl.DeviceIdType.MESH
HIGHEST = lax.Precision.HIGHEST
NT = (((1,), (1,)), ((), ()))


def dot_nt(a, b, precision=None):
    return lax.dot_general(a, b, NT, precision=precision, preferred_element_type=F32)


def factor(gram_wide):
    row = lax.broadcasted_iota(jnp.int32, (RANK, 2 * RANK), 0)
    lane = lax.broadcasted_iota(jnp.int32, (RANK, 2 * RANK), 1)
    work = gram_wide + jnp.where(row == lane, 1.0, 0.0)

    def step(j, w):
        pivot_row = jnp.sum(jnp.where(row == j, w, 0.0), axis=0, keepdims=True)
        column = jnp.sum(jnp.where(lane == j + RANK, w, 0.0), axis=1, keepdims=True)
        pivot = jnp.sum(jnp.where(lane[:1] == j + RANK, pivot_row, 0.0), axis=1, keepdims=True)
        ratio = jnp.where(row[:, :1] > j, column, 0.0) / pivot
        return w - ratio * pivot_row

    work = lax.fori_loop(0, RANK, step, work)
    diagonal = jnp.sum(jnp.where(lane == row + RANK, work, 0.0), axis=1, keepdims=True)
    return work * lax.rsqrt(diagonal)


def subspace_kernel(d_hbm, b_ref, left_ref, right_ref, mid_ref, d, ag, y, rs, g, dsem, ssem, rsem):
    me = lax.axis_index("rows")

    def peer_of(k):
        return lax.rem(me + k, N)

    def copy_to(src, dst, phase, k):
        return pltpu.make_async_remote_copy(
            src_ref=src,
            dst_ref=dst,
            send_sem=ssem.at[phase, k],
            recv_sem=rsem.at[phase, me],
            device_id={"rows": peer_of(k)},
            device_id_type=MESH,
        )

    def arrival(buffer, phase, source):
        pltpu.make_async_remote_copy(
            src_ref=buffer,
            dst_ref=buffer,
            send_sem=ssem.at[phase, 0],
            recv_sem=rsem.at[phase, source],
            device_id={"rows": source},
            device_id_type=MESH,
        ).wait_recv()

    load = pltpu.make_async_copy(d_hbm, d, dsem)
    load.start()

    barrier = pltpu.get_barrier_semaphore()

    @pl.loop(1, N)
    def _(k):
        pl.semaphore_signal(barrier, inc=1, device_id={"rows": peer_of(k)}, device_id_type=MESH)

    pl.semaphore_wait(barrier, N - 1)

    def columns(j):
        return pl.ds(pl.multiple_of(j * COLS, 128), COLS)

    def gather_start(sweep, phase):
        src = b_ref if sweep == 0 else ag.at[1, me]

        @pl.loop(1, N)
        def _(k):
            copy_to(src, ag.at[sweep, me], phase, k).start()

    def left_product(sweep, phase):
        own = b_ref[...] if sweep == 0 else ag[1, me]
        total = dot_nt(own, d[:, columns(me)])

        def step(k, total):
            source = lax.rem(me + N - k, N)
            arrival(ag.at[sweep, source], phase, source)
            return total + dot_nt(ag[sweep, source], d[:, columns(source)])

        return lax.fori_loop(1, N, step, total)

    def gram_start(raw, index, phase):
        wide = jnp.concatenate([jnp.zeros_like(raw), raw], axis=0)
        g[index, me] = dot_nt(raw, wide, HIGHEST)

        @pl.loop(1, N)
        def _(k):
            copy_to(g.at[index, me], g.at[index, me], phase, k).start()

    def gram_factor(index, phase):
        @pl.loop(1, N)
        def _(k):
            source = lax.rem(me + N - k, N)
            arrival(g.at[index, source], phase, source)

        total = g[index, 0]
        for source in range(1, N):
            total = total + g[index, source]
        return factor(total)

    def scatter_start(left16, sweep, phase):
        @pl.loop(1, N)
        def _(k):
            j = peer_of(k)
            y[sweep, j] = jnp.dot(left16, d[:, columns(j)], preferred_element_type=F32).astype(BF)
            copy_to(y.at[sweep, j], rs.at[sweep, me], phase, k).start()

        y[sweep, me] = jnp.dot(left16, d[:, columns(me)], preferred_element_type=F32).astype(BF)

    def scatter_sum(sweep, phase):
        def step(k, total):
            source = lax.rem(me + N - k, N)
            arrival(rs.at[sweep, source], phase, source)
            return total + rs[sweep, source].astype(F32)

        return lax.fori_loop(1, N, step, y[sweep, me].astype(F32))

    gather_start(0, 0)
    load.wait()
    left_raw = left_product(0, 0)
    gram_start(left_raw, 0, 1)
    scatter_start(left_raw.astype(BF), 0, 2)
    left_fact = gram_factor(0, 1)
    right_raw = jnp.dot(left_fact[:, :RANK], scatter_sum(0, 2), precision=HIGHEST)
    gram_start(right_raw, 1, 3)
    ag[1, me] = right_raw.astype(BF)
    gather_start(1, 4)
    right_fact = gram_factor(1, 3)
    left_raw = jnp.dot(right_fact[:, :RANK], left_product(1, 4), precision=HIGHEST)
    gram_start(left_raw, 2, 5)
    scatter_start(left_raw.astype(BF), 1, 6)
    left_fact = gram_factor(2, 5)
    left_ref[...] = jnp.dot(left_fact[:, :RANK], left_raw, precision=HIGHEST).astype(BF)
    right_raw = jnp.dot(left_fact[:, :RANK], scatter_sum(1, 6), precision=HIGHEST)
    gram_start(right_raw, 3, 7)
    right_fact = gram_factor(3, 7)
    mid_ref[...] = right_fact
    right_ref[...] = jnp.dot(right_fact[:, :RANK], right_raw, precision=HIGHEST).astype(BF)

    @pl.loop(1, N)
    def _(k):
        for sweep, phase in ((0, 0), (1, 4)):
            copy_to(ag.at[sweep, me], ag.at[sweep, me], phase, k).wait_send()
        for index, phase in ((0, 1), (1, 3), (2, 5), (3, 7)):
            copy_to(g.at[index, me], g.at[index, me], phase, k).wait_send()
        for sweep, phase in ((0, 2), (1, 6)):
            copy_to(y.at[sweep, me], rs.at[sweep, me], phase, k).wait_send()


def subspace(changes, start_t):
    rows = changes.shape[0]
    vmem = pl.BlockSpec(memory_space=pltpu.VMEM)
    return pl.pallas_call(
        subspace_kernel,
        out_shape=(
            jax.ShapeDtypeStruct((RANK, rows), BF),
            jax.ShapeDtypeStruct((RANK, COLS), BF),
            jax.ShapeDtypeStruct((RANK, 2 * RANK), F32),
        ),
        in_specs=[pl.BlockSpec(memory_space=pl.ANY), vmem],
        out_specs=(vmem, vmem, vmem),
        scratch_shapes=[
            pltpu.VMEM((rows, N * COLS), BF),
            pltpu.VMEM((2, N, RANK, COLS), BF),
            pltpu.VMEM((2, N, RANK, COLS), BF),
            pltpu.VMEM((2, N, RANK, COLS), BF),
            pltpu.VMEM((4, N, RANK, 2 * RANK), F32),
            pltpu.SemaphoreType.DMA,
            pltpu.SemaphoreType.DMA((8, N)),
            pltpu.SemaphoreType.DMA((8, N)),
        ],
        compiler_params=pltpu.CompilerParams(
            collective_id=0, has_side_effects=True, vmem_limit_bytes=40 * 1024 * 1024
        ),
        name="subspace",
    )(changes, start_t)


def whitener(gram):
    def mul(a, b):
        return jnp.dot(a.astype(BF), b.astype(BF), preferred_element_type=F32)

    lead, tail = 1.5 / 4.0, -0.5 / 64.0
    product = lead * jnp.eye(N * RANK, dtype=F32) + tail * gram
    for step in range(NS_ITERS):
        if step > 0:
            lead, tail = 1.5, -0.5
            product = lead * product + tail * mul(product, gram)
        if step < NS_ITERS - 1:
            half = lead * gram + tail * mul(gram, gram)
            gram = lead * half + tail * mul(half, gram)
    return product.astype(BF)


def body(deltas, start_basis, edit_order):
    left_t, right_t, right_fact = subspace(deltas[0], start_basis[0].T)
    ckpt_index = lax.axis_index("ckpt")
    position = jnp.sum(jnp.where(jnp.arange(N) == ckpt_index, edit_order, 0))
    weight = (1 + position).astype(F32) / N
    middle = (right_fact[:, RANK:].T * weight).astype(BF)

    left_all = lax.all_gather(left_t, "ckpt", axis=0, tiled=True)
    swap = [(c * N + r, r * N + c) for c in range(N) for r in range(N)]
    right_swapped = lax.ppermute(right_t, ("ckpt", "rows"), swap)
    right_all = lax.all_gather(right_swapped, "rows", axis=0, tiled=True)
    gram_left = lax.psum(dot_nt(left_all, left_t).astype(BF), "rows")
    gram_right = lax.psum(dot_nt(right_all, right_swapped).astype(BF), "ckpt")
    gram_left = lax.all_gather(gram_left, "ckpt", axis=1, tiled=True).astype(F32)
    gram_right = lax.all_gather(gram_right, "rows", axis=1, tiled=True).astype(F32)
    middles = lax.all_gather(middle, "ckpt", axis=0, tiled=False)
    white_left = whitener(gram_left)
    white_right = whitener(gram_right)
    scaled = jnp.einsum(
        "kcr,crs->kcs", white_left.reshape(N * RANK, N, RANK), middles, preferred_element_type=F32
    ).reshape(N * RANK, N * RANK).astype(BF)
    scaled_left = lax.dot_general(
        left_all, scaled, (((0,), (0,)), ((), ())), preferred_element_type=F32
    ).astype(BF)
    right_white = jnp.dot(white_right, right_all, preferred_element_type=F32).astype(BF)
    return jnp.dot(scaled_left, right_white, preferred_element_type=F32).astype(BF)


def solution(mesh):
    return jax.shard_map(
        body,
        mesh=mesh,
        in_specs=(P("ckpt", "rows", None), P("ckpt", "rows", None), P()),
        out_specs=P("rows", "ckpt"),
        check_vma=False,
    )
```

```python
import jax
import jax.numpy as jnp
from jax import lax
from jax.experimental import pallas as pl
from jax.experimental.pallas import tpu as pltpu
from jax.sharding import PartitionSpec as P

RANK = 64
NS_ITERS = 4
N = 16
COLS = 896
ROWS = 256
PACK = ROWS + 2 * RANK
ALL = N * RANK
BF = jnp.bfloat16
F32 = jnp.float32
MESH = pl.DeviceIdType.MESH
HIGHEST = lax.Precision.HIGHEST
NT = (((1,), (1,)), ((), ()))


def dot_nt(a, b, precision=None):
    return lax.dot_general(a, b, NT, precision=precision, preferred_element_type=F32)


def factor(gram_wide):
    row = lax.broadcasted_iota(jnp.int32, (RANK, 2 * RANK), 0)
    lane = lax.broadcasted_iota(jnp.int32, (RANK, 2 * RANK), 1)
    work = gram_wide + jnp.where(row == lane, 1.0, 0.0)

    def step(j, w):
        pivot_row = jnp.sum(jnp.where(row == j, w, 0.0), axis=0, keepdims=True)
        column = jnp.sum(jnp.where(lane == j + RANK, w, 0.0), axis=1, keepdims=True)
        pivot = jnp.sum(jnp.where(lane[:1] == j + RANK, pivot_row, 0.0), axis=1, keepdims=True)
        ratio = jnp.where(row[:, :1] > j, column, 0.0) / pivot
        return w - ratio * pivot_row

    work = lax.fori_loop(0, RANK, step, work)
    diagonal = jnp.sum(jnp.where(lane == row + RANK, work, 0.0), axis=1, keepdims=True)
    return work * lax.rsqrt(diagonal)


def subspace_kernel(d_hbm, b_ref, pack_ref, right_ref, d, ag, y, rs, g, dsem, ssem, rsem):
    me = lax.axis_index("rows")

    def peer_of(k):
        return lax.rem(me + k, N)

    def copy_to(src, dst, phase, k):
        return pltpu.make_async_remote_copy(
            src_ref=src,
            dst_ref=dst,
            send_sem=ssem.at[phase, k],
            recv_sem=rsem.at[phase, me],
            device_id={"rows": peer_of(k)},
            device_id_type=MESH,
        )

    def arrival(buffer, phase, source):
        pltpu.make_async_remote_copy(
            src_ref=buffer,
            dst_ref=buffer,
            send_sem=ssem.at[phase, 0],
            recv_sem=rsem.at[phase, source],
            device_id={"rows": source},
            device_id_type=MESH,
        ).wait_recv()

    load = pltpu.make_async_copy(d_hbm, d, dsem)
    load.start()

    barrier = pltpu.get_barrier_semaphore()

    @pl.loop(1, N)
    def _(k):
        pl.semaphore_signal(barrier, inc=1, device_id={"rows": peer_of(k)}, device_id_type=MESH)

    pl.semaphore_wait(barrier, N - 1)

    def columns(j):
        return pl.ds(pl.multiple_of(j * COLS, 128), COLS)

    def gather_start(sweep, phase):
        src = b_ref if sweep == 0 else ag.at[1, me]

        @pl.loop(1, N)
        def _(k):
            copy_to(src, ag.at[sweep, me], phase, k).start()

    def left_product(sweep, phase):
        own = b_ref[...] if sweep == 0 else ag[1, me]
        total = dot_nt(own, d[:, columns(me)])

        def step(k, total):
            source = lax.rem(me + N - k, N)
            arrival(ag.at[sweep, source], phase, source)
            return total + dot_nt(ag[sweep, source], d[:, columns(source)])

        return lax.fori_loop(1, N, step, total)

    def gram_start(raw, index, phase):
        wide = jnp.concatenate([jnp.zeros_like(raw), raw], axis=0)
        g[index, me] = dot_nt(raw, wide, HIGHEST)

        @pl.loop(1, N)
        def _(k):
            copy_to(g.at[index, me], g.at[index, me], phase, k).start()

    def gram_factor(index, phase):
        @pl.loop(1, N)
        def _(k):
            source = lax.rem(me + N - k, N)
            arrival(g.at[index, source], phase, source)

        total = g[index, 0]
        for source in range(1, N):
            total = total + g[index, source]
        return factor(total)

    def scatter_start(left16, sweep, phase):
        @pl.loop(1, N)
        def _(k):
            j = peer_of(k)
            y[sweep, j] = jnp.dot(left16, d[:, columns(j)], preferred_element_type=F32).astype(BF)
            copy_to(y.at[sweep, j], rs.at[sweep, me], phase, k).start()

        y[sweep, me] = jnp.dot(left16, d[:, columns(me)], preferred_element_type=F32).astype(BF)

    def scatter_sum(sweep, phase):
        def step(k, total):
            source = lax.rem(me + N - k, N)
            arrival(rs.at[sweep, source], phase, source)
            return total + rs[sweep, source].astype(F32)

        return lax.fori_loop(1, N, step, y[sweep, me].astype(F32))

    gather_start(0, 0)
    load.wait()
    left_raw = left_product(0, 0)
    gram_start(left_raw, 0, 1)
    scatter_start(left_raw.astype(BF), 0, 2)
    left_fact = gram_factor(0, 1)
    right_raw = jnp.dot(left_fact[:, :RANK], scatter_sum(0, 2), precision=HIGHEST)
    gram_start(right_raw, 1, 3)
    ag[1, me] = right_raw.astype(BF)
    gather_start(1, 4)
    right_fact = gram_factor(1, 3)
    left_raw = jnp.dot(right_fact[:, :RANK], left_product(1, 4), precision=HIGHEST)
    gram_start(left_raw, 2, 5)
    scatter_start(left_raw.astype(BF), 1, 6)
    left_fact = gram_factor(2, 5)
    pack_ref[:, :ROWS] = jnp.dot(left_fact[:, :RANK], left_raw, precision=HIGHEST).astype(BF)
    right_raw = jnp.dot(left_fact[:, :RANK], scatter_sum(1, 6), precision=HIGHEST)
    gram_start(right_raw, 3, 7)
    right_fact = gram_factor(3, 7)
    pack_ref[:, ROWS:] = right_fact.astype(BF)
    right_ref[...] = jnp.dot(right_fact[:, :RANK], right_raw, precision=HIGHEST).astype(BF)

    @pl.loop(1, N)
    def _(k):
        for sweep, phase in ((0, 0), (1, 4)):
            copy_to(ag.at[sweep, me], ag.at[sweep, me], phase, k).wait_send()
        for index, phase in ((0, 1), (1, 3), (2, 5), (3, 7)):
            copy_to(g.at[index, me], g.at[index, me], phase, k).wait_send()
        for sweep, phase in ((0, 2), (1, 6)):
            copy_to(y.at[sweep, me], rs.at[sweep, me], phase, k).wait_send()


def subspace(changes, start_t):
    rows = changes.shape[0]
    vmem = pl.BlockSpec(memory_space=pltpu.VMEM)
    return pl.pallas_call(
        subspace_kernel,
        out_shape=(
            jax.ShapeDtypeStruct((RANK, PACK), BF),
            jax.ShapeDtypeStruct((RANK, COLS), BF),
        ),
        in_specs=[pl.BlockSpec(memory_space=pl.ANY), vmem],
        out_specs=(vmem, vmem),
        scratch_shapes=[
            pltpu.VMEM((rows, N * COLS), BF),
            pltpu.VMEM((2, N, RANK, COLS), BF),
            pltpu.VMEM((2, N, RANK, COLS), BF),
            pltpu.VMEM((2, N, RANK, COLS), BF),
            pltpu.VMEM((4, N, RANK, 2 * RANK), F32),
            pltpu.SemaphoreType.DMA,
            pltpu.SemaphoreType.DMA((8, N)),
            pltpu.SemaphoreType.DMA((8, N)),
        ],
        compiler_params=pltpu.CompilerParams(
            collective_id=0, has_side_effects=True, vmem_limit_bytes=40 * 1024 * 1024
        ),
        name="subspace",
    )(changes, start_t)


def gather_kernel(pack_ref, right_ref, lall, rall, gram, glp, grp, grs, blk, zst, lsem, ssem, rsem):
    c = lax.axis_index("ckpt")
    r = lax.axis_index("rows")

    def rows64(i):
        return pl.ds(pl.multiple_of(i * RANK, RANK), RANK)

    def rows32(i):
        return pl.ds(pl.multiple_of(i * 32, 32), 32)

    def tile_of(i):
        return (
            pl.ds(pl.multiple_of(lax.rem(i, 2) * 512, 512), 512),
            pl.ds(pl.multiple_of(lax.div(i, 2) * 128, 128), 128),
        )

    def send(axis, mine, src, dst, phase, k):
        return pltpu.make_async_remote_copy(
            src_ref=src,
            dst_ref=dst,
            send_sem=ssem.at[phase, k],
            recv_sem=rsem.at[phase, mine],
            device_id={axis: lax.rem(mine + k, N)},
            device_id_type=MESH,
        )

    def arrival(axis, buffer, phase, source):
        pltpu.make_async_remote_copy(
            src_ref=buffer,
            dst_ref=buffer,
            send_sem=ssem.at[phase, 0],
            recv_sem=rsem.at[phase, source],
            device_id={axis: source},
            device_id_type=MESH,
        ).wait_recv()

    def swap_copy():
        return pltpu.make_async_remote_copy(
            src_ref=right_ref,
            dst_ref=rall.at[rows64(r)],
            send_sem=ssem.at[7, 0],
            recv_sem=rsem.at[7, 0],
            device_id={"ckpt": r, "rows": c},
            device_id_type=MESH,
        )

    barrier = pltpu.get_barrier_semaphore()

    @pl.loop(1, N)
    def _(k):
        pl.semaphore_signal(barrier, inc=1, device_id={"ckpt": lax.rem(c + k, N)}, device_id_type=MESH)
        pl.semaphore_signal(barrier, inc=1, device_id={"rows": lax.rem(r + k, N)}, device_id_type=MESH)

    @pl.when(c != r)
    def _():
        pl.semaphore_signal(barrier, inc=1, device_id={"ckpt": r, "rows": c}, device_id_type=MESH)
        pl.semaphore_wait(barrier, 2 * N - 1)

    @pl.when(c == r)
    def _():
        pl.semaphore_wait(barrier, 2 * N - 2)

    @pl.when(c != r)
    def _():
        pltpu.make_async_remote_copy(
            src_ref=right_ref,
            dst_ref=rall.at[rows64(c)],
            send_sem=ssem.at[7, 0],
            recv_sem=rsem.at[7, 0],
            device_id={"ckpt": r, "rows": c},
            device_id_type=MESH,
        ).start()

    @pl.loop(1, N)
    def _(k):
        send("ckpt", c, pack_ref, lall.at[rows64(c)], 0, k).start()

    own = pltpu.make_async_copy(pack_ref, lall.at[rows64(c)], lsem.at[0])
    own.start()

    @pl.when(c != r)
    def _():
        swap_copy().wait_recv()

    @pl.when(c == r)
    def _():
        local = pltpu.make_async_copy(right_ref, rall.at[rows64(r)], lsem.at[1])
        local.start()
        local.wait()

    @pl.loop(1, N)
    def _(k):
        send("rows", r, rall.at[rows64(r)], rall.at[rows64(r)], 1, k).start()

    own.wait()

    @pl.loop(1, N)
    def _(k):
        source = lax.rem(c + N - k, N)
        arrival("ckpt", lall.at[rows64(source)], 0, source)

    left_all = lall[:, :ROWS]
    for half in range(2):
        strip = lall[pl.ds(pl.multiple_of(half * 512 + c * 32, 32), 32), :ROWS]
        part = dot_nt(strip, left_all).astype(BF)
        for q in range(8):
            glp[2 * q + half] = part[:, q * 128 : (q + 1) * 128]

    @pl.loop(1, N)
    def _(k):
        send("rows", r, glp.at[lax.rem(r + k, N)], grs.at[0, r], 2, k).start()

    @pl.loop(1, N)
    def _(k):
        source = lax.rem(r + N - k, N)
        arrival("rows", rall.at[rows64(source)], 1, source)

    half_rows, pair = tile_of(r)
    pair_rows = pl.ds(pl.multiple_of(lax.div(r, 2) * 128, 128), 128)
    grp[...] = dot_nt(rall[half_rows, :], rall[pair_rows, :]).astype(BF)

    @pl.loop(1, N)
    def _(k):
        send("ckpt", c, grp.at[rows32(lax.rem(c + k, N))], grs.at[1, c], 3, k).start()

    def total(axis, mine, side, phase, first):
        def step(k, value):
            source = lax.rem(mine + N - k, N)
            arrival(axis, grs.at[side, source], phase, source)
            return value + grs[side, source].astype(F32)

        return lax.fori_loop(1, N, step, first.astype(F32)).astype(BF)

    blk[0] = total("rows", r, 0, 2, glp[r])
    blk[1] = total("ckpt", c, 1, 3, grp[rows32(c)])

    @pl.loop(1, N)
    def _(k):
        send("ckpt", c, blk.at[lax.rem(c + k, 2)], zst.at[rows32(c)], 4, k).start()

    zst[rows32(c)] = blk[lax.rem(c, 2)]

    @pl.loop(1, N)
    def _(k):
        source = lax.rem(c + N - k, N)
        arrival("ckpt", zst.at[rows32(source)], 4, source)

    @pl.loop(1, N)
    def _(k):
        send("rows", r, zst, gram.at[half_rows, pair], 5, k).start()

    gram[half_rows, pair] = zst[...]

    @pl.loop(1, N)
    def _(k):
        source = lax.rem(r + N - k, N)
        arrival("rows", gram.at[tile_of(source)], 5, source)

    @pl.when(c != r)
    def _():
        swap_copy().wait_send()

    @pl.loop(1, N)
    def _(k):
        send("ckpt", c, pack_ref, lall.at[rows64(c)], 0, k).wait_send()
        send("rows", r, rall.at[rows64(r)], rall.at[rows64(r)], 1, k).wait_send()
        send("rows", r, glp.at[0], grs.at[0, r], 2, k).wait_send()
        send("ckpt", c, grp.at[rows32(c)], grs.at[1, c], 3, k).wait_send()
        send("ckpt", c, blk.at[0], zst.at[rows32(c)], 4, k).wait_send()
        send("rows", r, zst, gram.at[half_rows, pair], 5, k).wait_send()


def gather_stacks(pack, right_t):
    vmem = pl.BlockSpec(memory_space=pltpu.VMEM)
    return pl.pallas_call(
        gather_kernel,
        out_shape=(
            jax.ShapeDtypeStruct((ALL, PACK), BF),
            jax.ShapeDtypeStruct((ALL, COLS), BF),
            jax.ShapeDtypeStruct((ALL, ALL), BF),
        ),
        in_specs=[vmem, vmem],
        out_specs=(vmem, vmem, vmem),
        scratch_shapes=[
            pltpu.VMEM((N, 32, 128), BF),
            pltpu.VMEM((512, 128), BF),
            pltpu.VMEM((2, N, 32, 128), BF),
            pltpu.VMEM((2, 32, 128), BF),
            pltpu.VMEM((512, 128), BF),
            pltpu.SemaphoreType.DMA((2,)),
            pltpu.SemaphoreType.DMA((8, N)),
            pltpu.SemaphoreType.DMA((8, N)),
        ],
        compiler_params=pltpu.CompilerParams(
            collective_id=1, has_side_effects=True, vmem_limit_bytes=40 * 1024 * 1024
        ),
        name="gather_stacks",
    )(pack, right_t)


def merge_kernel(own, lall, rall, out, both, scaled, white, lsem, ssem, rsem):
    c = lax.axis_index("ckpt")
    side = lax.rem(c, 2)
    other = c + 1 - 2 * side
    barrier = pltpu.get_barrier_semaphore()
    pl.semaphore_signal(barrier, inc=1, device_id={"ckpt": other}, device_id_type=MESH)
    pl.semaphore_wait(barrier, 1)
    exchange = pltpu.make_async_remote_copy(
        src_ref=own,
        dst_ref=both.at[side],
        send_sem=ssem,
        recv_sem=rsem,
        device_id={"ckpt": other},
        device_id_type=MESH,
    )
    exchange.start()
    keep = pltpu.make_async_copy(own, both.at[side], lsem)
    keep.start()
    keep.wait()
    pltpu.make_async_remote_copy(
        src_ref=own,
        dst_ref=both.at[1 - side],
        send_sem=ssem,
        recv_sem=rsem,
        device_id={"ckpt": other},
        device_id_type=MESH,
    ).wait_recv()
    scaled[...] = lax.dot_general(
        lall[:, :ROWS], both[0], (((0,), (0,)), ((), ())), preferred_element_type=F32
    ).astype(BF)

    @pl.loop(0, 4)
    def _(i):
        part = pl.ds(pl.multiple_of(i * 256, 256), 256)
        white[part, :] = jnp.dot(both[1, part, :], rall[...], preferred_element_type=F32).astype(BF)

    out[...] = jnp.dot(scaled[...], white[...], preferred_element_type=F32).astype(BF)
    exchange.wait_send()


def merge(own, lall, rall):
    vmem = pl.BlockSpec(memory_space=pltpu.VMEM)
    return pl.pallas_call(
        merge_kernel,
        out_shape=jax.ShapeDtypeStruct((ROWS, COLS), BF),
        in_specs=[vmem, vmem, vmem],
        out_specs=vmem,
        scratch_shapes=[
            pltpu.VMEM((2, ALL, ALL), BF),
            pltpu.VMEM((ROWS, ALL), BF),
            pltpu.VMEM((ALL, COLS), BF),
            pltpu.SemaphoreType.DMA,
            pltpu.SemaphoreType.DMA,
            pltpu.SemaphoreType.DMA,
        ],
        compiler_params=pltpu.CompilerParams(
            collective_id=2, has_side_effects=True, vmem_limit_bytes=40 * 1024 * 1024
        ),
        name="merge",
    )(own, lall, rall)


def whitener(gram16):
    def mul(a, b):
        return jnp.dot(a.astype(BF), b.astype(BF), preferred_element_type=F32)

    gram = gram16.astype(F32)
    lead, tail = 1.5 / 4.0, -0.5 / 64.0
    product = lead * jnp.eye(ALL, dtype=F32) + tail * gram
    for step in range(NS_ITERS):
        if step > 0:
            lead, tail = 1.5, -0.5
            product = lead * product + tail * mul(product, gram)
        if step < NS_ITERS - 1:
            half = lead * gram + tail * mul(gram, gram)
            gram = lead * half + tail * mul(half, gram)
    return product.astype(BF)


def body(deltas, start_basis, edit_order):
    pack, right_t = subspace(deltas[0], start_basis[0].T)
    lall, rall, gram = gather_stacks(pack, right_t)
    white = whitener(gram)
    weights = jnp.repeat((1 + edit_order).astype(F32) / N, RANK)
    middle_t = lall[:, ROWS + RANK :].astype(F32) * weights[:, None]
    block = jnp.arange(ALL) // RANK
    same = block[:, None] == block[None, :]
    even = lax.rem(lax.axis_index("ckpt"), 2) == 0
    scale_t = jnp.where(
        even, jnp.where(same, jnp.tile(middle_t, (1, N)), 0.0), jnp.eye(ALL, dtype=F32)
    ).astype(BF)
    own = dot_nt(white, scale_t).astype(BF)
    return merge(own, lall, rall)


def solution(mesh):
    return jax.shard_map(
        body,
        mesh=mesh,
        in_specs=(P("ckpt", "rows", None), P("ckpt", "rows", None), P()),
        out_specs=P("rows", "ckpt"),
        check_vma=False,
    )
```

```python
import jax
import jax.numpy as jnp
from jax import lax
from jax.experimental import pallas as pl
from jax.experimental.pallas import tpu as pltpu
from jax.sharding import PartitionSpec as P

RANK = 64
NS_ITERS = 4
N = 16
COLS = 896
ROWS = 256
PACK = ROWS + 2 * RANK
ALL = N * RANK
TILE = 256
BF = jnp.bfloat16
F32 = jnp.float32
MESH = pl.DeviceIdType.MESH
HIGHEST = lax.Precision.HIGHEST
NT = (((1,), (1,)), ((), ()))


def dot_nt(a, b, precision=None):
    return lax.dot_general(a, b, NT, precision=precision, preferred_element_type=F32)


def factor(gram_wide):
    row = lax.broadcasted_iota(jnp.int32, (RANK, 2 * RANK), 0)
    lane = lax.broadcasted_iota(jnp.int32, (RANK, 2 * RANK), 1)
    work = gram_wide + jnp.where(row == lane, 1.0, 0.0)

    def step(j, w):
        pivot_row = jnp.sum(jnp.where(row == j, w, 0.0), axis=0, keepdims=True)
        column = jnp.sum(jnp.where(lane == j + RANK, w, 0.0), axis=1, keepdims=True)
        pivot = jnp.sum(jnp.where(lane[:1] == j + RANK, pivot_row, 0.0), axis=1, keepdims=True)
        ratio = jnp.where(row[:, :1] > j, column, 0.0) / pivot
        return w - ratio * pivot_row

    work = lax.fori_loop(0, RANK, step, work)
    diagonal = jnp.sum(jnp.where(lane == row + RANK, work, 0.0), axis=1, keepdims=True)
    return work * lax.rsqrt(diagonal)


OFFSETS = (0, -1, 1, 2)
FAR_FIRST = (2, 1, -1, 0)


class Plane:
    def __init__(self, ssem, rsem):
        self.ssem, self.rsem = ssem, rsem
        self.r = lax.axis_index("rows")
        self.x, self.y = lax.rem(self.r, 4), lax.div(self.r, 4)
        self.sends = []

    def place(self, axis, da, db):
        dx, dy = (da, db) if axis == 0 else (db, da)
        return lax.rem(self.y + dy + 4, 4) * 4 + lax.rem(self.x + dx + 4, 4)

    def spot(self, axis, delta):
        return lax.rem((self.x if axis == 0 else self.y) + delta + 4, 4)

    def copy(self, src, dst, sem, to):
        return pltpu.make_async_remote_copy(
            src_ref=src,
            dst_ref=dst,
            send_sem=self.ssem.at[sem],
            recv_sem=self.rsem.at[sem],
            device_id={"rows": to},
            device_id_type=MESH,
        )

    def go(self, src, dst, sem, to):
        copy = self.copy(src, dst, sem, to)
        copy.start()
        self.sends.append(copy)

    def got(self, dst, sem):
        self.copy(dst, dst, sem, self.r).wait_recv()

    def finish(self):
        for copy in self.sends:
            copy.wait_send()

    def gather(self, half, quarter, base, ready):
        def send(ref, h, slot, da, db):
            self.go(ref, ref, base + 20 * h + slot, self.place(h, da, db))

        def take(ref, h, slot):
            self.got(ref, base + 20 * h + slot)

        def spread(h, j):
            origin = self.place(h, OFFSETS[j], 0)
            send(half(h, origin), h, 4 + j, 0, 1)
            send(half(h, origin), h, 8 + j, 0, -1)

        def relay(h, j):
            origin = self.place(h, OFFSETS[j], -1)
            take(half(h, origin), h, 4 + j)
            send(quarter(h, origin, 0), h, 12 + j, 0, 1)
            origin = self.place(h, OFFSETS[j], 1)
            take(half(h, origin), h, 8 + j)
            send(quarter(h, origin, 1), h, 16 + j, 0, -1)

        for h in range(2):
            send(half(h, self.r), h, 0, 1, 0)
            send(half(h, self.r), h, 1, -1, 0)
            spread(h, 0)
        ready([(0, 0)])
        for h in range(2):
            origin = self.place(h, -1, 0)
            take(half(h, origin), h, 0)
            send(quarter(h, origin, 0), h, 2, 1, 0)
            origin = self.place(h, 1, 0)
            take(half(h, origin), h, 1)
            send(quarter(h, origin, 1), h, 3, -1, 0)
        for h in range(2):
            spread(h, 1)
            spread(h, 2)
        for h in range(2):
            relay(h, 0)
        for h in range(2):
            origin = self.place(h, 2, 0)
            take(quarter(h, origin, 0), h, 2)
            take(quarter(h, origin, 1), h, 3)
            spread(h, 3)
        ready([(-1, 0), (1, 0), (0, -1), (0, 1)])
        for j in (1, 2):
            for h in range(2):
                relay(h, j)
        ready([(-1, -1), (1, -1), (-1, 1), (1, 1)])
        for h in range(2):
            relay(h, 3)
        groups = ([(0, 2), (2, 0)], [(-1, 2), (2, -1)], [(1, 2), (2, 1)], [(2, 2)])
        for j in range(4):
            for h in range(2):
                origin = self.place(h, OFFSETS[j], 2)
                take(quarter(h, origin, 0), h, 12 + j)
                take(quarter(h, origin, 1), h, 16 + j)
            ready(groups[j])

    def scatter(self, part, y, t1, t2, s1, u1, u2, base, between):
        done = set()

        def make(dx, dy):
            if (dx, dy) in done:
                return
            done.add((dx, dy))
            xs, ys = self.spot(0, dx), self.spot(1, dy)
            value = part(ys * 4 + xs).astype(BF)
            y[0, ys, xs] = value[:32]
            y[1, xs, ys] = value[32:]

        def low(q):
            return pl.ds(16 * q, 16)

        for i, j in enumerate(FAR_FIRST):
            for h in range(2):
                make(*((j, 2) if h == 0 else (2, j)))
                b, a = self.spot(1 - h, 2), self.spot(h, j)
                for q in range(2):
                    self.go(
                        y.at[h, b, a, low(q)], t1.at[h, q, i], base + 20 * h + 4 * q + i,
                        self.place(h, 0, 1 - 2 * q),
                    )
        between()
        for i, j in enumerate(FAR_FIRST):
            for h in range(2):
                for q in range(2):
                    delta = 1 - 2 * q
                    make(*((j, delta) if h == 0 else (delta, j)))
                    b, a = self.spot(1 - h, delta), self.spot(h, j)
                    self.got(t1.at[h, q, i], base + 20 * h + 4 * q + i)
                    y[h, b, a, low(q)] = (
                        y[h, b, a, low(q)].astype(F32) + t1[h, q, i].astype(F32)
                    ).astype(BF)
                    self.go(
                        y.at[h, b, a], t2.at[h, q, i], base + 20 * h + 8 + 4 * q + i,
                        self.place(h, 0, delta),
                    )
        make(0, 0)
        result = [None, None]
        for i, j in enumerate(FAR_FIRST):
            for h in range(2):
                b, a = self.spot(1 - h, 0), self.spot(h, j)
                make(*((j, 0) if h == 0 else (0, j)))
                self.got(t2.at[h, 0, i], base + 20 * h + 8 + i)
                self.got(t2.at[h, 1, i], base + 20 * h + 12 + i)
                total = y[h, b, a].astype(F32) + t2[h, 0, i].astype(F32) + t2[h, 1, i].astype(F32)
                if j == 2:
                    s1[h, i] = total.astype(BF)
                    for q in range(2):
                        self.go(
                            s1.at[h, i, low(q)], u1.at[h, q], base + 20 * h + 16 + q,
                            self.place(h, 1 - 2 * q, 0),
                        )
                elif j != 0:
                    q = 0 if j == 1 else 1
                    self.got(u1.at[h, q], base + 20 * h + 16 + q)
                    s1[h, i] = total.astype(BF)
                    s1[h, i, low(q)] = (
                        total[16 * q : 16 * q + 16] + u1[h, q].astype(F32)
                    ).astype(BF)
                    self.go(
                        s1.at[h, i], u2.at[h, q], base + 20 * h + 18 + q, self.place(h, j, 0)
                    )
                else:
                    result[h] = total
        for h in range(2):
            for q in range(2):
                self.got(u2.at[h, q], base + 20 * h + 18 + q)
                result[h] = result[h] + u2[h, q].astype(F32)
        return jnp.concatenate(result, axis=0)


def subspace_kernel(
    d_hbm, b_ref, pack_ref, right_ref, d, ag, y, t1, t2, s1, u1, u2, gx, gy, dsem, ssem, rsem
):
    plane = Plane(ssem, rsem)
    me = plane.r
    load = pltpu.make_async_copy(d_hbm, d, dsem)
    load.start()
    barrier = pltpu.get_barrier_semaphore()

    @pl.loop(1, N)
    def _(k):
        pl.semaphore_signal(barrier, inc=1, device_id={"rows": lax.rem(me + k, N)}, device_id_type=MESH)

    ag[0, me] = b_ref[...]
    pl.semaphore_wait(barrier, N - 1)

    def columns(j):
        return pl.ds(pl.multiple_of(j * COLS, 128), COLS)

    def left_product(sweep, base, between):
        total = [jnp.zeros((RANK, ROWS), F32)]

        def ready(sources):
            for dx, dy in sources:
                source = plane.place(0, dx, dy)
                if (dx, dy) == (0, 0) and sweep == 0:
                    load.wait()
                total[0] = total[0] + dot_nt(ag[sweep, source], d[:, columns(source)])
            if len(sources) == 4 and sources[0] == (-1, 0):
                between()

        plane.gather(
            lambda h, o: ag.at[sweep, o, pl.ds(32 * h, 32)],
            lambda h, o, q: ag.at[sweep, o, pl.ds(32 * h + 16 * q, 16)],
            base,
            ready,
        )
        return total[0]

    def right_product(left16, sweep, base, between):
        return plane.scatter(
            lambda j: jnp.dot(left16, d[:, columns(j)], preferred_element_type=F32),
            *(ref.at[sweep] for ref in (y, t1, t2, s1, u1, u2)),
            base,
            between,
        )

    def exchange(buffer, axis, base):
        mine = plane.spot(axis, 0)
        for k in range(1, 4):
            plane.go(buffer.at[mine], buffer.at[mine], base + k, plane.place(axis, k, 0))

    def collect(buffer, axis, base):
        for k in range(1, 4):
            plane.got(buffer.at[plane.spot(axis, -k)], base + k)
        return (buffer[0] + buffer[1]) + (buffer[2] + buffer[3])

    def gram_start(raw, index):
        wide = dot_nt(raw, jnp.concatenate([jnp.zeros_like(raw), raw], axis=0), HIGHEST)
        gx[index, plane.x] = pltpu.roll(wide[:32], RANK, 1) + wide[32:]
        exchange(gx.at[index], 0, 160 + 8 * index)

    def gram_middle(index):
        gy[index, plane.y] = collect(gx.at[index], 0, 160 + 8 * index)
        exchange(gy.at[index], 1, 164 + 8 * index)

    def gram_factor(index):
        total = collect(gy.at[index], 1, 164 + 8 * index)
        right = lax.broadcasted_iota(jnp.int32, (32, 128), 1) >= RANK
        upper = jnp.where(right, pltpu.roll(total, RANK, 1), 0.0)
        lower = jnp.where(right, total, 0.0)
        return factor(jnp.concatenate([upper, lower], axis=0))

    left_raw = left_product(0, 0, lambda: None)
    gram_start(left_raw, 0)
    facts = {}

    def left_between(index):
        gram_middle(index)
        facts[index] = gram_factor(index)

    right_sum = right_product(left_raw.astype(BF), 0, 80, lambda: left_between(0))
    right_raw = jnp.dot(facts[0][:, :RANK], right_sum, precision=HIGHEST)
    ag[1, me] = right_raw.astype(BF)

    def right_between(index):
        gram_middle(index)
        facts[index] = gram_factor(index)

    gram_start(right_raw, 1)
    left_product_1 = left_product(1, 40, lambda: right_between(1))
    left_raw = jnp.dot(facts[1][:, :RANK], left_product_1, precision=HIGHEST)
    gram_start(left_raw, 2)
    right_sum = right_product(left_raw.astype(BF), 1, 120, lambda: left_between(2))
    right_raw = jnp.dot(facts[2][:, :RANK], right_sum, precision=HIGHEST)
    gram_start(right_raw, 3)
    pack_ref[:, :ROWS] = jnp.dot(facts[2][:, :RANK], left_raw, precision=HIGHEST).astype(BF)
    gram_middle(3)
    right_fact = gram_factor(3)
    pack_ref[:, ROWS:] = pltpu.roll(right_fact, RANK, 1).astype(BF)
    right_ref[...] = jnp.dot(right_fact[:, :RANK], right_raw, precision=HIGHEST).astype(BF)
    plane.finish()


def subspace(changes, start_t):
    rows = changes.shape[0]
    vmem = pl.BlockSpec(memory_space=pltpu.VMEM)
    return pl.pallas_call(
        subspace_kernel,
        out_shape=(
            jax.ShapeDtypeStruct((RANK, PACK), BF),
            jax.ShapeDtypeStruct((RANK, COLS), BF),
        ),
        in_specs=[pl.BlockSpec(memory_space=pl.ANY), vmem],
        out_specs=(vmem, vmem),
        scratch_shapes=[
            pltpu.VMEM((rows, N * COLS), BF),
            pltpu.VMEM((2, N, RANK, COLS), BF),
            pltpu.VMEM((2, 2, 4, 4, 32, COLS), BF),
            pltpu.VMEM((2, 2, 2, 4, 16, COLS), BF),
            pltpu.VMEM((2, 2, 2, 4, 32, COLS), BF),
            pltpu.VMEM((2, 2, 4, 32, COLS), BF),
            pltpu.VMEM((2, 2, 2, 16, COLS), BF),
            pltpu.VMEM((2, 2, 2, 32, COLS), BF),
            pltpu.VMEM((4, 4, 32, 128), F32),
            pltpu.VMEM((4, 4, 32, 128), F32),
            pltpu.SemaphoreType.DMA,
            pltpu.SemaphoreType.DMA((192,)),
            pltpu.SemaphoreType.DMA((192,)),
        ],
        compiler_params=pltpu.CompilerParams(
            collective_id=0, has_side_effects=True, vmem_limit_bytes=60 * 1024 * 1024
        ),
        name="subspace",
    )(changes, start_t)


def gather_kernel(pack_ref, right_ref, lall, rall, gram, glp, grp, grs, blk, zst, lsem, ssem, rsem):
    c = lax.axis_index("ckpt")
    r = lax.axis_index("rows")

    def rows64(i):
        return pl.ds(pl.multiple_of(i * RANK, RANK), RANK)

    def rows32(i):
        return pl.ds(pl.multiple_of(i * 32, 32), 32)

    def tile_of(i):
        return (
            pl.ds(pl.multiple_of(lax.rem(i, 2) * 512, 512), 512),
            pl.ds(pl.multiple_of(lax.div(i, 2) * 128, 128), 128),
        )

    def send(axis, mine, src, dst, phase, k):
        return pltpu.make_async_remote_copy(
            src_ref=src,
            dst_ref=dst,
            send_sem=ssem.at[phase, k],
            recv_sem=rsem.at[phase, mine],
            device_id={axis: lax.rem(mine + k, N)},
            device_id_type=MESH,
        )

    def arrival(axis, buffer, phase, source):
        pltpu.make_async_remote_copy(
            src_ref=buffer,
            dst_ref=buffer,
            send_sem=ssem.at[phase, 0],
            recv_sem=rsem.at[phase, source],
            device_id={axis: source},
            device_id_type=MESH,
        ).wait_recv()

    def swap_copy():
        return pltpu.make_async_remote_copy(
            src_ref=right_ref,
            dst_ref=rall.at[rows64(r)],
            send_sem=ssem.at[7, 0],
            recv_sem=rsem.at[7, 0],
            device_id={"ckpt": r, "rows": c},
            device_id_type=MESH,
        )

    barrier = pltpu.get_barrier_semaphore()

    @pl.loop(1, N)
    def _(k):
        pl.semaphore_signal(barrier, inc=1, device_id={"ckpt": lax.rem(c + k, N)}, device_id_type=MESH)
        pl.semaphore_signal(barrier, inc=1, device_id={"rows": lax.rem(r + k, N)}, device_id_type=MESH)

    @pl.when(c != r)
    def _():
        pl.semaphore_signal(barrier, inc=1, device_id={"ckpt": r, "rows": c}, device_id_type=MESH)
        pl.semaphore_wait(barrier, 2 * N - 1)

    @pl.when(c == r)
    def _():
        pl.semaphore_wait(barrier, 2 * N - 2)

    @pl.when(c != r)
    def _():
        pltpu.make_async_remote_copy(
            src_ref=right_ref,
            dst_ref=rall.at[rows64(c)],
            send_sem=ssem.at[7, 0],
            recv_sem=rsem.at[7, 0],
            device_id={"ckpt": r, "rows": c},
            device_id_type=MESH,
        ).start()

    @pl.loop(1, N)
    def _(k):
        send("ckpt", c, pack_ref, lall.at[rows64(c)], 0, k).start()

    own = pltpu.make_async_copy(pack_ref, lall.at[rows64(c)], lsem.at[0])
    own.start()

    @pl.when(c != r)
    def _():
        swap_copy().wait_recv()

    @pl.when(c == r)
    def _():
        local = pltpu.make_async_copy(right_ref, rall.at[rows64(r)], lsem.at[1])
        local.start()
        local.wait()

    @pl.loop(1, N)
    def _(k):
        send("rows", r, rall.at[rows64(r)], rall.at[rows64(r)], 1, k).start()

    own.wait()

    @pl.loop(1, N)
    def _(k):
        source = lax.rem(c + N - k, N)
        arrival("ckpt", lall.at[rows64(source)], 0, source)

    left_all = lall[:, :ROWS]
    for half in range(2):
        strip = lall[pl.ds(pl.multiple_of(half * 512 + c * 32, 32), 32), :ROWS]
        part = dot_nt(strip, left_all).astype(BF)
        for q in range(8):
            glp[2 * q + half] = part[:, q * 128 : (q + 1) * 128]

    @pl.loop(1, N)
    def _(k):
        send("rows", r, glp.at[lax.rem(r + k, N)], grs.at[0, r], 2, k).start()

    @pl.loop(1, N)
    def _(k):
        source = lax.rem(r + N - k, N)
        arrival("rows", rall.at[rows64(source)], 1, source)

    half_rows, pair = tile_of(r)
    pair_rows = pl.ds(pl.multiple_of(lax.div(r, 2) * 128, 128), 128)
    grp[...] = dot_nt(rall[half_rows, :], rall[pair_rows, :]).astype(BF)

    @pl.loop(1, N)
    def _(k):
        send("ckpt", c, grp.at[rows32(lax.rem(c + k, N))], grs.at[1, c], 3, k).start()

    def total(axis, mine, side, phase, first):
        def step(k, value):
            source = lax.rem(mine + N - k, N)
            arrival(axis, grs.at[side, source], phase, source)
            return value + grs[side, source].astype(F32)

        return lax.fori_loop(1, N, step, first.astype(F32)).astype(BF)

    blk[0] = total("rows", r, 0, 2, glp[r])
    blk[1] = total("ckpt", c, 1, 3, grp[rows32(c)])

    @pl.loop(1, N)
    def _(k):
        send("ckpt", c, blk.at[lax.rem(c + k, 2)], zst.at[rows32(c)], 4, k).start()

    zst[rows32(c)] = blk[lax.rem(c, 2)]

    @pl.loop(1, N)
    def _(k):
        source = lax.rem(c + N - k, N)
        arrival("ckpt", zst.at[rows32(source)], 4, source)

    @pl.loop(1, N)
    def _(k):
        send("rows", r, zst, gram.at[half_rows, pair], 5, k).start()

    gram[half_rows, pair] = zst[...]

    @pl.loop(1, N)
    def _(k):
        source = lax.rem(r + N - k, N)
        arrival("rows", gram.at[tile_of(source)], 5, source)

    @pl.when(c != r)
    def _():
        swap_copy().wait_send()

    @pl.loop(1, N)
    def _(k):
        send("ckpt", c, pack_ref, lall.at[rows64(c)], 0, k).wait_send()
        send("rows", r, rall.at[rows64(r)], rall.at[rows64(r)], 1, k).wait_send()
        send("rows", r, glp.at[0], grs.at[0, r], 2, k).wait_send()
        send("ckpt", c, grp.at[rows32(c)], grs.at[1, c], 3, k).wait_send()
        send("ckpt", c, blk.at[0], zst.at[rows32(c)], 4, k).wait_send()
        send("rows", r, zst, gram.at[half_rows, pair], 5, k).wait_send()


def gather_stacks(pack, right_t):
    vmem = pl.BlockSpec(memory_space=pltpu.VMEM)
    return pl.pallas_call(
        gather_kernel,
        out_shape=(
            jax.ShapeDtypeStruct((ALL, PACK), BF),
            jax.ShapeDtypeStruct((ALL, COLS), BF),
            jax.ShapeDtypeStruct((ALL, ALL), BF),
        ),
        in_specs=[vmem, vmem],
        out_specs=(vmem, vmem, vmem),
        scratch_shapes=[
            pltpu.VMEM((N, 32, 128), BF),
            pltpu.VMEM((512, 128), BF),
            pltpu.VMEM((2, N, 32, 128), BF),
            pltpu.VMEM((2, 32, 128), BF),
            pltpu.VMEM((512, 128), BF),
            pltpu.SemaphoreType.DMA((2,)),
            pltpu.SemaphoreType.DMA((8, N)),
            pltpu.SemaphoreType.DMA((8, N)),
        ],
        compiler_params=pltpu.CompilerParams(
            collective_id=1, has_side_effects=True, vmem_limit_bytes=40 * 1024 * 1024
        ),
        name="gather_stacks",
    )(pack, right_t)


def merge_kernel(gram, lall, rall, order, out, chain, half, left, right, scaled, ssem, rsem):
    c = lax.axis_index("ckpt")
    side = lax.rem(c, 2)
    even = side == 0
    other = c + 1 - 2 * side

    def to_other(src, dst, sem):
        return pltpu.make_async_remote_copy(
            src_ref=src,
            dst_ref=dst,
            send_sem=ssem.at[sem],
            recv_sem=rsem.at[sem],
            device_id={"ckpt": other},
            device_id_type=MESH,
        )

    barrier = pltpu.get_barrier_semaphore()
    pl.semaphore_signal(barrier, inc=1, device_id={"ckpt": other}, device_id_type=MESH)
    pl.semaphore_wait(barrier, 1)

    @pl.when(~even)
    def _():
        to_other(gram, chain.at[1, 0], 0).start()

    def factors(step):
        return (1.5 / 4.0, -0.5 / 64.0) if step == 0 else (1.5, -0.5)

    def advance(dst, old, weights, lead, tail, tile):
        @pl.loop(0, ALL // tile)
        def _(i):
            part = pl.ds(pl.multiple_of(i * tile, tile), tile)
            product = jnp.dot(old[part, :], weights[...], preferred_element_type=F32)
            dst[part, :] = (lead * old[part, :].astype(F32) + tail * product).astype(BF)

    def apply(dst, old, grams, lead, tail, tile):
        @pl.loop(0, ALL // tile)
        def _(i):
            part = pl.ds(pl.multiple_of(i * tile, tile), tile)
            product = jnp.dot(grams[part, :], old[...], preferred_element_type=F32)
            dst[part, :] = (lead * old[part, :].astype(F32) + tail * product).astype(BF)

    for step in range(NS_ITERS - 1):
        current = gram if step == 0 else chain.at[side, step]
        advance(half, current, current, *factors(step), TILE)
        advance(chain.at[side, step + 1], half, current, *factors(step), TILE)

        @pl.when(~even)
        def _():
            to_other(chain.at[1, step + 1], chain.at[1, step + 1], step + 1).start()

    @pl.when(even)
    def _():
        for step in range(NS_ITERS):
            old = lall.at[:, :ROWS] if step == 0 else left.at[(step - 1) % 2]
            current = gram if step == 0 else chain.at[0, step]
            apply(left.at[step % 2], old, current, *factors(step), TILE)
        for k in range(N):
            block = pl.ds(k * RANK, RANK)
            weight = (1 + order[k]).astype(F32) / N
            middle_t = lall[block, ROWS : ROWS + RANK]
            scaled[block, :] = (
                weight * jnp.dot(middle_t, left[(NS_ITERS - 1) % 2, block, :], preferred_element_type=F32)
            ).astype(BF)
        to_other(scaled, scaled, 4).start()
        for step in range(NS_ITERS):
            to_other(chain.at[1, step], chain.at[1, step], step).wait_recv()
            old = rall if step == 0 else right.at[(step - 1) % 2]
            apply(right.at[step % 2], old, chain.at[1, step], *factors(step), TILE)
        to_other(scaled, scaled, 4).wait_send()

    @pl.when(~even)
    def _():
        for step in range(NS_ITERS):
            old = rall if step == 0 else right.at[(step - 1) % 2]
            current = gram if step == 0 else chain.at[1, step]
            apply(right.at[step % 2], old, current, *factors(step), TILE)
        for step in range(NS_ITERS):
            to_other(chain.at[1, step], chain.at[1, step], step).wait_send()
        to_other(scaled, scaled, 4).wait_recv()

    out[...] = lax.dot_general(
        scaled[...], right[(NS_ITERS - 1) % 2], (((0,), (0,)), ((), ())), preferred_element_type=F32
    ).astype(BF)


def merge(gram, lall, rall, edit_order):
    vmem = pl.BlockSpec(memory_space=pltpu.VMEM)
    return pl.pallas_call(
        merge_kernel,
        out_shape=jax.ShapeDtypeStruct((ROWS, COLS), BF),
        in_specs=[vmem, vmem, vmem, pl.BlockSpec(memory_space=pltpu.SMEM)],
        out_specs=vmem,
        scratch_shapes=[
            pltpu.VMEM((2, NS_ITERS, ALL, ALL), BF),
            pltpu.VMEM((ALL, ALL), BF),
            pltpu.VMEM((2, ALL, ROWS), BF),
            pltpu.VMEM((2, ALL, COLS), BF),
            pltpu.VMEM((ALL, ROWS), BF),
            pltpu.SemaphoreType.DMA((5,)),
            pltpu.SemaphoreType.DMA((5,)),
        ],
        compiler_params=pltpu.CompilerParams(
            collective_id=2, has_side_effects=True, vmem_limit_bytes=45 * 1024 * 1024
        ),
        name="merge",
    )(gram, lall, rall, edit_order)


def body(deltas, start_basis, edit_order):
    pack, right_t = subspace(deltas[0], start_basis[0].T)
    lall, rall, gram = gather_stacks(pack, right_t)
    return merge(gram, lall, rall, edit_order)


def solution(mesh):
    return jax.shard_map(
        body,
        mesh=mesh,
        in_specs=(P("ckpt", "rows", None), P("ckpt", "rows", None), P()),
        out_specs=P("rows", "ckpt"),
        check_vma=False,
    )
```

```python
import functools

import jax
import jax.numpy as jnp
from jax import lax
from jax.experimental import pallas as pl
from jax.experimental.pallas import tpu as pltpu
from jax.sharding import PartitionSpec as P

RANK = 64
NS_ITERS = 4
N = 16
COLS = 896
ROWS = 256
PACK = ROWS + 2 * RANK
ALL = N * RANK
TILE = 256
BF = jnp.bfloat16
F32 = jnp.float32
MESH = pl.DeviceIdType.MESH
HIGHEST = lax.Precision.HIGHEST
NT = (((1,), (1,)), ((), ()))


def dot_nt(a, b, precision=None):
    return lax.dot_general(a, b, NT, precision=precision, preferred_element_type=F32)


def factor_start(gram_wide):
    row = lax.broadcasted_iota(jnp.int32, (RANK, 2 * RANK), 0)
    lane = lax.broadcasted_iota(jnp.int32, (RANK, 2 * RANK), 1)
    return gram_wide + jnp.where(row == lane, 1.0, 0.0)


def factor_steps(work, first, last):
    row = lax.broadcasted_iota(jnp.int32, (RANK, 2 * RANK), 0)
    lane = lax.broadcasted_iota(jnp.int32, (RANK, 2 * RANK), 1)

    def step(j, w):
        pivot_row = jnp.sum(jnp.where(row == j, w, 0.0), axis=0, keepdims=True)
        column = jnp.sum(jnp.where(lane == j + RANK, w, 0.0), axis=1, keepdims=True)
        pivot = jnp.sum(jnp.where(lane[:1] == j + RANK, pivot_row, 0.0), axis=1, keepdims=True)
        ratio = jnp.where(row[:, :1] > j, column, 0.0) / pivot
        return w - ratio * pivot_row

    return lax.fori_loop(first, last, step, work)


def factor_end(work):
    row = lax.broadcasted_iota(jnp.int32, (RANK, 2 * RANK), 0)
    lane = lax.broadcasted_iota(jnp.int32, (RANK, 2 * RANK), 1)
    diagonal = jnp.sum(jnp.where(lane == row + RANK, work, 0.0), axis=1, keepdims=True)
    return work * lax.rsqrt(diagonal)


def xor(a, b):
    return sum(bit * lax.rem(lax.div(a, bit) + lax.div(b, bit), 2) for bit in (1, 2, 4, 8))


OFFSETS = (0, -1, 1, 2)
FAR_FIRST = (2, 1, -1, 0)


class Plane:
    def __init__(self, ssem, rsem):
        self.ssem, self.rsem = ssem, rsem
        self.r = lax.axis_index("rows")
        self.x, self.y = lax.rem(self.r, 4), lax.div(self.r, 4)
        self.sends = []
        self.tasks = []

    def place(self, axis, da, db):
        dx, dy = (da, db) if axis == 0 else (db, da)
        return lax.rem(self.y + dy + 4, 4) * 4 + lax.rem(self.x + dx + 4, 4)

    def spot(self, axis, delta):
        return lax.rem((self.x if axis == 0 else self.y) + delta + 4, 4)

    def copy(self, src, dst, sem, to):
        return pltpu.make_async_remote_copy(
            src_ref=src,
            dst_ref=dst,
            send_sem=self.ssem.at[sem],
            recv_sem=self.rsem.at[sem],
            device_id={"rows": to},
            device_id_type=MESH,
        )

    def go(self, src, dst, sem, to):
        copy = self.copy(src, dst, sem, to)
        copy.start()
        self.sends.append(copy)

    def got(self, dst, sem):
        self.copy(dst, dst, sem, self.r).wait_recv()

    def tick(self):
        if self.tasks:
            self.tasks.pop(0)()

    def flush(self):
        while self.tasks:
            self.tick()

    def finish(self):
        for copy in self.sends:
            copy.wait_send()

    def gather(self, half, quarter, base, ready):
        def send(ref, h, slot, da, db):
            self.go(ref, ref, base + 20 * h + slot, self.place(h, da, db))

        def take(ref, h, slot):
            self.got(ref, base + 20 * h + slot)

        def spread(h, j):
            origin = self.place(h, OFFSETS[j], 0)
            send(half(h, origin), h, 4 + j, 0, 1)
            send(half(h, origin), h, 8 + j, 0, -1)

        def relay(h, j):
            origin = self.place(h, OFFSETS[j], -1)
            take(half(h, origin), h, 4 + j)
            send(quarter(h, origin, 0), h, 12 + j, 0, 1)
            origin = self.place(h, OFFSETS[j], 1)
            take(half(h, origin), h, 8 + j)
            send(quarter(h, origin, 1), h, 16 + j, 0, -1)

        for h in range(2):
            send(half(h, self.r), h, 0, 1, 0)
            send(half(h, self.r), h, 1, -1, 0)
            spread(h, 0)
        ready([(0, 0)])
        self.tick()
        for h in range(2):
            origin = self.place(h, -1, 0)
            take(half(h, origin), h, 0)
            send(quarter(h, origin, 0), h, 2, 1, 0)
            origin = self.place(h, 1, 0)
            take(half(h, origin), h, 1)
            send(quarter(h, origin, 1), h, 3, -1, 0)
        for h in range(2):
            spread(h, 1)
            spread(h, 2)
        self.tick()
        for h in range(2):
            relay(h, 0)
        for h in range(2):
            origin = self.place(h, 2, 0)
            take(quarter(h, origin, 0), h, 2)
            take(quarter(h, origin, 1), h, 3)
            spread(h, 3)
        ready([(-1, 0), (1, 0), (0, -1), (0, 1)])
        self.tick()
        for j in (1, 2):
            for h in range(2):
                relay(h, j)
        self.tick()
        ready([(-1, -1), (1, -1), (-1, 1), (1, 1)])
        for h in range(2):
            relay(h, 3)
        self.tick()
        groups = ([(0, 2), (2, 0)], [(-1, 2), (2, -1)], [(1, 2), (2, 1)], [(2, 2)])
        for j in range(4):
            for h in range(2):
                origin = self.place(h, OFFSETS[j], 2)
                take(quarter(h, origin, 0), h, 12 + j)
                take(quarter(h, origin, 1), h, 16 + j)
            ready(groups[j])
        self.flush()

    def scatter(self, part, y, t1, t2, s1, u1, u2, base):
        done = set()

        def make(dx, dy):
            if (dx, dy) in done:
                return
            done.add((dx, dy))
            xs, ys = self.spot(0, dx), self.spot(1, dy)
            value = part(ys * 4 + xs).astype(BF)
            y[0, ys, xs] = value[:32]
            y[1, xs, ys] = value[32:]

        def low(q):
            return pl.ds(16 * q, 16)

        for i, j in enumerate(FAR_FIRST):
            for h in range(2):
                make(*((j, 2) if h == 0 else (2, j)))
                b, a = self.spot(1 - h, 2), self.spot(h, j)
                for q in range(2):
                    self.go(
                        y.at[h, b, a, low(q)], t1.at[h, q, i], base + 20 * h + 4 * q + i,
                        self.place(h, 0, 1 - 2 * q),
                    )
        self.tick()
        for i, j in enumerate(FAR_FIRST):
            for h in range(2):
                for q in range(2):
                    delta = 1 - 2 * q
                    make(*((j, delta) if h == 0 else (delta, j)))
                    b, a = self.spot(1 - h, delta), self.spot(h, j)
                    self.got(t1.at[h, q, i], base + 20 * h + 4 * q + i)
                    y[h, b, a, low(q)] = (
                        y[h, b, a, low(q)].astype(F32) + t1[h, q, i].astype(F32)
                    ).astype(BF)
                    self.go(
                        y.at[h, b, a], t2.at[h, q, i], base + 20 * h + 8 + 4 * q + i,
                        self.place(h, 0, delta),
                    )
            self.tick()
        make(0, 0)
        self.flush()
        result = [None, None]
        for i, j in enumerate(FAR_FIRST):
            for h in range(2):
                b, a = self.spot(1 - h, 0), self.spot(h, j)
                make(*((j, 0) if h == 0 else (0, j)))
                self.got(t2.at[h, 0, i], base + 20 * h + 8 + i)
                self.got(t2.at[h, 1, i], base + 20 * h + 12 + i)
                total = y[h, b, a].astype(F32) + t2[h, 0, i].astype(F32) + t2[h, 1, i].astype(F32)
                if j == 2:
                    s1[h, i] = total.astype(BF)
                    for q in range(2):
                        self.go(
                            s1.at[h, i, low(q)], u1.at[h, q], base + 20 * h + 16 + q,
                            self.place(h, 1 - 2 * q, 0),
                        )
                elif j != 0:
                    q = 0 if j == 1 else 1
                    self.got(u1.at[h, q], base + 20 * h + 16 + q)
                    s1[h, i] = total.astype(BF)
                    s1[h, i, low(q)] = (
                        total[16 * q : 16 * q + 16] + u1[h, q].astype(F32)
                    ).astype(BF)
                    self.go(
                        s1.at[h, i], u2.at[h, q], base + 20 * h + 18 + q, self.place(h, j, 0)
                    )
                else:
                    result[h] = total
        for h in range(2):
            for q in range(2):
                self.got(u2.at[h, q], base + 20 * h + 18 + q)
                result[h] = result[h] + u2[h, q].astype(F32)
        return jnp.concatenate(result, axis=0)


def merge_kernel(
    d_hbm, b_ref, order, out,
    d, ag, y, t1, t2, s1, u1, u2, gx, gy,
    lall, fall, swp, raw, rall, gram, glp, grp, grs, blk, zst,
    chain, half, left, right, scaled,
    dsem, ssem, rsem, cs, cr, ssem2, rsem2,
):
    plane = Plane(ssem, rsem)
    me = r = plane.r
    c = lax.axis_index("ckpt")
    side = lax.rem(c, 2)
    even = side == 0
    other = c + 1 - 2 * side
    load = pltpu.make_async_copy(d_hbm, d, dsem.at[0])
    load.start()
    barrier = pltpu.get_barrier_semaphore()

    @pl.loop(1, N)
    def _(k):
        pl.semaphore_signal(barrier, inc=1, device_id={"rows": lax.rem(r + k, N)}, device_id_type=MESH)
        pl.semaphore_signal(barrier, inc=1, device_id={"ckpt": lax.rem(c + k, N)}, device_id_type=MESH)

    ag[0, me] = b_ref[...]
    pl.semaphore_wait(barrier, 2 * N - 2)

    def columns(j):
        return pl.ds(pl.multiple_of(j * COLS, 128), COLS)

    def left_product(sweep, base):
        total = [jnp.zeros((RANK, ROWS), F32)]

        def ready(sources):
            for dx, dy in sources:
                source = plane.place(0, dx, dy)
                if (dx, dy) == (0, 0) and sweep == 0:
                    load.wait()
                total[0] = total[0] + dot_nt(ag[sweep, source], d[:, columns(source)])

        plane.gather(
            lambda h, o: ag.at[sweep, o, pl.ds(32 * h, 32)],
            lambda h, o, q: ag.at[sweep, o, pl.ds(32 * h + 16 * q, 16)],
            base,
            ready,
        )
        return total[0]

    def right_product(left16, sweep, base, label):
        return plane.scatter(
            lambda j: jnp.dot(left16, d[:, columns(label(j))], preferred_element_type=F32),
            *(ref.at[sweep] for ref in (y, t1, t2, s1, u1, u2)),
            base,
        )

    def exchange(buffer, axis, base):
        mine = plane.spot(axis, 0)
        for k in range(1, 4):
            plane.go(buffer.at[mine], buffer.at[mine], base + k, plane.place(axis, k, 0))

    def collect(buffer, axis, base):
        for k in range(1, 4):
            plane.got(buffer.at[plane.spot(axis, -k)], base + k)
        return (buffer[0] + buffer[1]) + (buffer[2] + buffer[3])

    facts = {}

    def gram_start(value, index):
        wide = dot_nt(value, jnp.concatenate([jnp.zeros_like(value), value], axis=0), HIGHEST)
        gx[index, plane.x] = pltpu.roll(wide[:32], RANK, 1) + wide[32:]
        exchange(gx.at[index], 0, 160 + 8 * index)

        def middle():
            gy[index, plane.y] = collect(gx.at[index], 0, 160 + 8 * index)
            exchange(gy.at[index], 1, 164 + 8 * index)

        def begin():
            total = collect(gy.at[index], 1, 164 + 8 * index)
            on_right = lax.broadcasted_iota(jnp.int32, (32, 128), 1) >= RANK
            upper = jnp.where(on_right, pltpu.roll(total, RANK, 1), 0.0)
            lower = jnp.where(on_right, total, 0.0)
            work = factor_start(jnp.concatenate([upper, lower], axis=0))
            facts[index] = factor_steps(work, 0, 16)

        def go_on(first):
            facts[index] = factor_steps(facts[index], first, first + 16)
            if first == 48:
                facts[index] = factor_end(facts[index])

        plane.tasks = [middle, begin] + [functools.partial(go_on, first) for first in (16, 32, 48)]

    def apply_inverse(index, value):
        return jnp.dot(facts[index][:, :RANK], value, precision=HIGHEST)

    left_raw = left_product(0, 0)
    gram_start(left_raw, 0)
    right_sum = right_product(left_raw.astype(BF), 0, 80, lambda j: j)
    right_raw = apply_inverse(0, right_sum)
    ag[1, me] = right_raw.astype(BF)
    gram_start(right_raw, 1)
    left_raw = apply_inverse(1, left_product(1, 40))
    gram_start(left_raw, 2)
    right_raw = apply_inverse(2, right_product(left_raw.astype(BF), 1, 120, lambda j: xor(j, c)))

    def rows64(i):
        return pl.ds(pl.multiple_of(i * RANK, RANK), RANK)

    def rows32(i):
        return pl.ds(pl.multiple_of(i * 32, 32), 32)

    def tile_of(i):
        return lax.rem(i, 2) * 512, pl.ds(pl.multiple_of(lax.div(i, 2) * 128, 128), 128)

    def send(axis, mine, src, dst, phase, k):
        return pltpu.make_async_remote_copy(
            src_ref=src,
            dst_ref=dst,
            send_sem=cs.at[phase, k],
            recv_sem=cr.at[phase, mine],
            device_id={axis: lax.rem(mine + k, N)},
            device_id_type=MESH,
        )

    def arrival(axis, buffer, phase, source):
        pltpu.make_async_remote_copy(
            src_ref=buffer,
            dst_ref=buffer,
            send_sem=cs.at[phase, 0],
            recv_sem=cr.at[phase, source],
            device_id={axis: source},
            device_id_type=MESH,
        ).wait_recv()

    def swap():
        return pltpu.make_async_remote_copy(
            src_ref=swp,
            dst_ref=raw.at[r],
            send_sem=cs.at[5, 0],
            recv_sem=cr.at[5, 0],
            device_id={"ckpt": xor(r, c)},
            device_id_type=MESH,
        )

    right16 = right_raw.astype(BF)

    @pl.when(r == 0)
    def _():
        raw[0] = right16

    @pl.when(r != 0)
    def _():
        swp[...] = right16
        pltpu.make_async_remote_copy(
            src_ref=swp,
            dst_ref=raw.at[r],
            send_sem=cs.at[5, 0],
            recv_sem=cr.at[5, 0],
            device_id={"ckpt": xor(r, c)},
            device_id_type=MESH,
        ).start()

    gram_start(right_raw, 3)
    lall[rows64(c)] = apply_inverse(2, left_raw).astype(BF)

    @pl.loop(1, N)
    def _(k):
        send("ckpt", c, lall.at[rows64(c)], lall.at[rows64(c)], 0, k).start()

    plane.tick()

    def finish_fact():
        fall[rows64(c)] = facts[3].astype(BF)

        @pl.loop(1, N)
        def _(k):
            send("ckpt", c, fall.at[rows64(c)], fall.at[rows64(c)], 1, k).start()

    def left_gram():
        @pl.loop(1, N)
        def _(k):
            source = lax.rem(c + N - k, N)
            arrival("ckpt", lall.at[rows64(source)], 0, source)

        for part in range(2):
            strip = lall[pl.ds(pl.multiple_of(part * 512 + c * 32, 32), 32), :]
            product = dot_nt(strip, lall[...]).astype(BF)
            for q in range(8):
                glp[2 * q + part] = product[:, q * 128 : (q + 1) * 128]

        @pl.loop(1, N)
        def _(k):
            send("rows", r, glp.at[lax.rem(r + k, N)], grs.at[0, r], 2, k).start()

    plane.tasks = plane.tasks + [finish_fact, left_gram]

    @pl.when(r != 0)
    def _():
        swap().wait_recv()

    plane.gather(
        lambda h, o: raw.at[o, pl.ds(32 * h, 32)],
        lambda h, o, q: raw.at[o, pl.ds(32 * h + 16 * q, 16)],
        192,
        lambda sources: None,
    )

    @pl.loop(1, N)
    def _(k):
        source = lax.rem(c + N - k, N)
        arrival("ckpt", fall.at[rows64(source)], 1, source)

    @pl.loop(0, N)
    def _(o):
        e = xor(o, c)
        rall[rows64(e), :] = jnp.dot(
            fall[rows64(e), :RANK], raw[o], preferred_element_type=F32
        ).astype(BF)

    first_row, pair = tile_of(r)
    pair_rows = pl.ds(pl.multiple_of(lax.div(r, 2) * 128, 128), 128)
    half_rows = pl.ds(pl.multiple_of(first_row, 512), 512)
    grp[...] = dot_nt(rall[half_rows, :], rall[pair_rows, :]).astype(BF)

    @pl.loop(1, N)
    def _(k):
        send("ckpt", c, grp.at[rows32(lax.rem(c + k, N))], grs.at[1, c], 3, k).start()

    def total_of(axis, mine, which, phase, first):
        def step(k, value):
            source = lax.rem(mine + N - k, N)
            arrival(axis, grs.at[which, source], phase, source)
            return value + grs[which, source].astype(F32)

        return lax.fori_loop(1, N, step, first.astype(F32)).astype(BF)

    blk[0] = total_of("rows", r, 0, 2, glp[r])
    blk[1] = total_of("ckpt", c, 1, 3, grp[rows32(c)])

    @pl.loop(1, N)
    def _(k):
        send("ckpt", c, blk.at[lax.rem(c + k, 2)], zst.at[rows32(c)], 4, k).start()

    zst[rows32(c)] = blk[side]

    @pl.loop(1, N)
    def _(k):
        source = lax.rem(c + N - k, N)
        arrival("ckpt", zst.at[rows32(source)], 4, source)

    gram[half_rows, pair] = zst[...]

    def gram_part(o, start, size):
        row, lanes = tile_of(o)
        return gram.at[pl.ds(pl.multiple_of(row + start, 128), size), lanes]

    plane.gather(
        lambda h, o: gram_part(o, 256 * h, 256),
        lambda h, o, q: gram_part(o, 256 * h + 128 * q, 128),
        232,
        lambda sources: None,
    )

    def to_other(src, dst, sem):
        return pltpu.make_async_remote_copy(
            src_ref=src,
            dst_ref=dst,
            send_sem=ssem2.at[sem],
            recv_sem=rsem2.at[sem],
            device_id={"ckpt": other},
            device_id_type=MESH,
        )

    @pl.when(~even)
    def _():
        to_other(gram, chain.at[1, 0], 0).start()

    def factors(step):
        return (1.5 / 4.0, -0.5 / 64.0) if step == 0 else (1.5, -0.5)

    def advance(dst, old, weights, lead, tail, tile):
        @pl.loop(0, ALL // tile)
        def _(i):
            part = pl.ds(pl.multiple_of(i * tile, tile), tile)
            product = jnp.dot(old[part, :], weights[...], preferred_element_type=F32)
            dst[part, :] = (lead * old[part, :].astype(F32) + tail * product).astype(BF)

    def apply(dst, old, grams, lead, tail, tile):
        @pl.loop(0, ALL // tile)
        def _(i):
            part = pl.ds(pl.multiple_of(i * tile, tile), tile)
            product = jnp.dot(grams[part, :], old[...], preferred_element_type=F32)
            dst[part, :] = (lead * old[part, :].astype(F32) + tail * product).astype(BF)

    for step in range(NS_ITERS - 1):
        current = gram if step == 0 else chain.at[side, step]
        advance(half, current, current, *factors(step), TILE)
        advance(chain.at[side, step + 1], half, current, *factors(step), TILE)

        @pl.when(~even)
        def _():
            to_other(chain.at[1, step + 1], chain.at[1, step + 1], step + 1).start()

    @pl.when(even)
    def _():
        for step in range(NS_ITERS):
            old = lall if step == 0 else left.at[(step - 1) % 2]
            current = gram if step == 0 else chain.at[0, step]
            apply(left.at[step % 2], old, current, *factors(step), TILE)
        for k in range(N):
            block = pl.ds(k * RANK, RANK)
            weight = (1 + order[k]).astype(F32) / N
            white = left[(NS_ITERS - 1) % 2, block, :]
            white = jnp.concatenate([jnp.zeros_like(white), white], axis=0)
            scaled[block, :] = (
                weight * jnp.dot(fall[block, :], white, preferred_element_type=F32)
            ).astype(BF)
        to_other(scaled, scaled, 4).start()
        for step in range(NS_ITERS):
            to_other(chain.at[1, step], chain.at[1, step], step).wait_recv()
            old = rall if step == 0 else right.at[(step - 1) % 2]
            apply(right.at[step % 2], old, chain.at[1, step], *factors(step), TILE)
        to_other(scaled, scaled, 4).wait_send()

    @pl.when(~even)
    def _():
        for step in range(NS_ITERS):
            old = rall if step == 0 else right.at[(step - 1) % 2]
            current = gram if step == 0 else chain.at[1, step]
            apply(right.at[step % 2], old, current, *factors(step), TILE)
        for step in range(NS_ITERS):
            to_other(chain.at[1, step], chain.at[1, step], step).wait_send()
        to_other(scaled, scaled, 4).wait_recv()

    out[...] = lax.dot_general(
        scaled[...], right[(NS_ITERS - 1) % 2], (((0,), (0,)), ((), ())), preferred_element_type=F32
    ).astype(BF)

    @pl.when(r != 0)
    def _():
        swap().wait_send()

    @pl.loop(1, N)
    def _(k):
        send("ckpt", c, lall.at[rows64(c)], lall.at[rows64(c)], 0, k).wait_send()
        send("ckpt", c, fall.at[rows64(c)], fall.at[rows64(c)], 1, k).wait_send()
        send("rows", r, glp.at[0], grs.at[0, r], 2, k).wait_send()
        send("ckpt", c, grp.at[rows32(c)], grs.at[1, c], 3, k).wait_send()
        send("ckpt", c, blk.at[0], zst.at[rows32(c)], 4, k).wait_send()

    plane.finish()


def body(deltas, start_basis, edit_order):
    vmem = pl.BlockSpec(memory_space=pltpu.VMEM)
    return pl.pallas_call(
        merge_kernel,
        out_shape=jax.ShapeDtypeStruct((ROWS, COLS), BF),
        in_specs=[
            pl.BlockSpec(memory_space=pl.ANY), vmem, pl.BlockSpec(memory_space=pltpu.SMEM),
        ],
        out_specs=vmem,
        scratch_shapes=[
            pltpu.VMEM((ROWS, N * COLS), BF),
            pltpu.VMEM((2, N, RANK, COLS), BF),
            pltpu.VMEM((2, 2, 4, 4, 32, COLS), BF),
            pltpu.VMEM((2, 2, 2, 4, 16, COLS), BF),
            pltpu.VMEM((2, 2, 2, 4, 32, COLS), BF),
            pltpu.VMEM((2, 2, 4, 32, COLS), BF),
            pltpu.VMEM((2, 2, 2, 16, COLS), BF),
            pltpu.VMEM((2, 2, 2, 32, COLS), BF),
            pltpu.VMEM((4, 4, 32, 128), F32),
            pltpu.VMEM((4, 4, 32, 128), F32),
            pltpu.VMEM((ALL, ROWS), BF),
            pltpu.VMEM((ALL, 2 * RANK), BF),
            pltpu.VMEM((RANK, COLS), BF),
            pltpu.VMEM((N, RANK, COLS), BF),
            pltpu.VMEM((ALL, COLS), BF),
            pltpu.VMEM((ALL, ALL), BF),
            pltpu.VMEM((N, 32, 128), BF),
            pltpu.VMEM((512, 128), BF),
            pltpu.VMEM((2, N, 32, 128), BF),
            pltpu.VMEM((2, 32, 128), BF),
            pltpu.VMEM((512, 128), BF),
            pltpu.VMEM((2, NS_ITERS, ALL, ALL), BF),
            pltpu.VMEM((ALL, ALL), BF),
            pltpu.VMEM((2, ALL, ROWS), BF),
            pltpu.VMEM((2, ALL, COLS), BF),
            pltpu.VMEM((ALL, ROWS), BF),
            pltpu.SemaphoreType.DMA((1,)),
            pltpu.SemaphoreType.DMA((272,)),
            pltpu.SemaphoreType.DMA((272,)),
            pltpu.SemaphoreType.DMA((6, N)),
            pltpu.SemaphoreType.DMA((6, N)),
            pltpu.SemaphoreType.DMA((5,)),
            pltpu.SemaphoreType.DMA((5,)),
        ],
        compiler_params=pltpu.CompilerParams(
            collective_id=0, has_side_effects=True, vmem_limit_bytes=62 * 1024 * 1024
        ),
        name="merge",
    )(deltas[0], start_basis[0].T, edit_order)


def solution(mesh):
    return jax.shard_map(
        body,
        mesh=mesh,
        in_specs=(P("ckpt", "rows", None), P("ckpt", "rows", None), P()),
        out_specs=P("rows", "ckpt"),
        check_vma=False,
    )
```

```python
import functools

import jax
import jax.numpy as jnp
from jax import lax
from jax.experimental import pallas as pl
from jax.experimental.pallas import tpu as pltpu
from jax.sharding import PartitionSpec as P

RANK = 64
NS_ITERS = 4
N = 16
COLS = 896
ROWS = 256
PACK = ROWS + 2 * RANK
ALL = N * RANK
TILE = 512
PIVOTS = 4
BF = jnp.bfloat16
F32 = jnp.float32
MESH = pl.DeviceIdType.MESH
HIGHEST = lax.Precision.HIGHEST
NT = (((1,), (1,)), ((), ()))


def dot_nt(a, b, precision=None):
    return lax.dot_general(a, b, NT, precision=precision, preferred_element_type=F32)


def factor_start(gram_wide):
    row = lax.broadcasted_iota(jnp.int32, (RANK, 2 * RANK), 0)
    lane = lax.broadcasted_iota(jnp.int32, (RANK, 2 * RANK), 1)
    return gram_wide + jnp.where(row == lane, 1.0, 0.0)


def factor_steps(work, first, last):
    row = lax.broadcasted_iota(jnp.int32, (RANK, 2 * RANK), 0)
    lane = lax.broadcasted_iota(jnp.int32, (RANK, 2 * RANK), 1)

    def step(i, w):
        p = [PIVOTS * i + k for k in range(PIVOTS)]
        rows = [jnp.sum(jnp.where(row == p[k], w, 0.0), axis=0, keepdims=True) for k in range(PIVOTS)]
        cols = [
            jnp.sum(jnp.where(lane == p[k] + RANK, w, 0.0), axis=1, keepdims=True)
            for k in range(PIVOTS)
        ]
        block = {
            (k, m): jnp.sum(jnp.where(lane[:1] == p[m] + RANK, rows[k], 0.0), axis=1, keepdims=True)
            for k in range(PIVOTS)
            for m in range(k, PIVOTS)
        }
        inverse = []
        for k in range(PIVOTS):
            inverse.append(1.0 / block[k, k])
            for n in range(k + 1, PIVOTS):
                ratio = block[k, n] * inverse[k]
                rows[n] = rows[n] - ratio * rows[k]
                for m in range(n, PIVOTS):
                    block[n, m] = block[n, m] - ratio * block[k, m]
        for k in range(PIVOTS):
            ratio = jnp.where(row[:, :1] > p[k], cols[k], 0.0) * inverse[k]
            for m in range(k + 1, PIVOTS):
                cols[m] = cols[m] - ratio * block[k, m]
            w = w - ratio * rows[k]
        return w

    return lax.fori_loop(first // PIVOTS, last // PIVOTS, step, work)


def factor_end(work):
    row = lax.broadcasted_iota(jnp.int32, (RANK, 2 * RANK), 0)
    lane = lax.broadcasted_iota(jnp.int32, (RANK, 2 * RANK), 1)
    diagonal = jnp.sum(jnp.where(lane == row + RANK, work, 0.0), axis=1, keepdims=True)
    return work * lax.rsqrt(diagonal)


def xor(a, b):
    return sum(bit * lax.rem(lax.div(a, bit) + lax.div(b, bit), 2) for bit in (1, 2, 4, 8))


OFFSETS = (0, -1, 1, 2)
FAR_FIRST = (2, 1, -1, 0)


class Plane:
    def __init__(self, ssem, rsem):
        self.ssem, self.rsem = ssem, rsem
        self.r = lax.axis_index("rows")
        self.x, self.y = lax.rem(self.r, 4), lax.div(self.r, 4)
        self.sends = []
        self.tasks = []

    def place(self, axis, da, db):
        dx, dy = (da, db) if axis == 0 else (db, da)
        return lax.rem(self.y + dy + 4, 4) * 4 + lax.rem(self.x + dx + 4, 4)

    def spot(self, axis, delta):
        return lax.rem((self.x if axis == 0 else self.y) + delta + 4, 4)

    def copy(self, src, dst, sem, to):
        return pltpu.make_async_remote_copy(
            src_ref=src,
            dst_ref=dst,
            send_sem=self.ssem.at[sem],
            recv_sem=self.rsem.at[sem],
            device_id={"rows": to},
            device_id_type=MESH,
        )

    def go(self, src, dst, sem, to):
        copy = self.copy(src, dst, sem, to)
        copy.start()
        self.sends.append(copy)

    def got(self, dst, sem):
        self.copy(dst, dst, sem, self.r).wait_recv()

    def tick(self):
        if self.tasks:
            self.tasks.pop(0)()

    def flush(self):
        while self.tasks:
            self.tick()

    def finish(self):
        for copy in self.sends:
            copy.wait_send()

    def gather(self, half, quarter, base, ready, landed=None):
        def send(ref, h, slot, da, db):
            self.go(ref, ref, base + 20 * h + slot, self.place(h, da, db))

        def take(ref, h, slot):
            self.got(ref, base + 20 * h + slot)

        def spread(h, j):
            origin = self.place(h, OFFSETS[j], 0)
            send(half(h, origin), h, 4 + j, 0, 1)
            send(half(h, origin), h, 8 + j, 0, -1)

        def relay(h, j):
            origin = self.place(h, OFFSETS[j], -1)
            take(half(h, origin), h, 4 + j)
            send(quarter(h, origin, 0), h, 12 + j, 0, 1)
            origin = self.place(h, OFFSETS[j], 1)
            take(half(h, origin), h, 8 + j)
            send(quarter(h, origin, 1), h, 16 + j, 0, -1)

        for h in range(2):
            if landed is not None:
                landed(h)
            send(half(h, self.r), h, 0, 1, 0)
            send(half(h, self.r), h, 1, -1, 0)
            spread(h, 0)
        ready([(0, 0)])
        self.tick()
        for h in range(2):
            origin = self.place(h, -1, 0)
            take(half(h, origin), h, 0)
            send(quarter(h, origin, 0), h, 2, 1, 0)
            origin = self.place(h, 1, 0)
            take(half(h, origin), h, 1)
            send(quarter(h, origin, 1), h, 3, -1, 0)
        for h in range(2):
            spread(h, 1)
            spread(h, 2)
        self.tick()
        for h in range(2):
            relay(h, 0)
        for h in range(2):
            origin = self.place(h, 2, 0)
            take(quarter(h, origin, 0), h, 2)
            take(quarter(h, origin, 1), h, 3)
            spread(h, 3)
        ready([(-1, 0), (1, 0), (0, -1), (0, 1)])
        self.tick()
        for j in (1, 2):
            for h in range(2):
                relay(h, j)
        self.tick()
        ready([(-1, -1), (1, -1), (-1, 1), (1, 1)])
        for h in range(2):
            relay(h, 3)
        self.tick()
        groups = ([(0, 2), (2, 0)], [(-1, 2), (2, -1)], [(1, 2), (2, 1)], [(2, 2)])
        for j in range(4):
            for h in range(2):
                origin = self.place(h, OFFSETS[j], 2)
                take(quarter(h, origin, 0), h, 12 + j)
                take(quarter(h, origin, 1), h, 16 + j)
            ready(groups[j])
        self.flush()

    def scatter(self, part, y, t1, t2, s1, u1, u2, base):
        done = set()

        def make(dx, dy):
            if (dx, dy) in done:
                return
            done.add((dx, dy))
            xs, ys = self.spot(0, dx), self.spot(1, dy)
            value = part(ys * 4 + xs).astype(BF)
            y[0, ys, xs] = value[:32]
            y[1, xs, ys] = value[32:]

        def low(q):
            return pl.ds(16 * q, 16)

        for i, j in enumerate(FAR_FIRST):
            for h in range(2):
                make(*((j, 2) if h == 0 else (2, j)))
                b, a = self.spot(1 - h, 2), self.spot(h, j)
                for q in range(2):
                    self.go(
                        y.at[h, b, a, low(q)], t1.at[h, q, i], base + 20 * h + 4 * q + i,
                        self.place(h, 0, 1 - 2 * q),
                    )
        self.tick()
        for i, j in enumerate(FAR_FIRST):
            for h in range(2):
                for q in range(2):
                    delta = 1 - 2 * q
                    make(*((j, delta) if h == 0 else (delta, j)))
                    b, a = self.spot(1 - h, delta), self.spot(h, j)
                    self.got(t1.at[h, q, i], base + 20 * h + 4 * q + i)
                    y[h, b, a, low(q)] = (
                        y[h, b, a, low(q)].astype(F32) + t1[h, q, i].astype(F32)
                    ).astype(BF)
                    self.go(
                        y.at[h, b, a], t2.at[h, q, i], base + 20 * h + 8 + 4 * q + i,
                        self.place(h, 0, delta),
                    )
            self.tick()
        make(0, 0)
        self.flush()
        result = [None, None]
        for i, j in enumerate(FAR_FIRST):
            for h in range(2):
                b, a = self.spot(1 - h, 0), self.spot(h, j)
                make(*((j, 0) if h == 0 else (0, j)))
                self.got(t2.at[h, 0, i], base + 20 * h + 8 + i)
                self.got(t2.at[h, 1, i], base + 20 * h + 12 + i)
                total = y[h, b, a].astype(F32) + t2[h, 0, i].astype(F32) + t2[h, 1, i].astype(F32)
                if j == 2:
                    s1[h, i] = total.astype(BF)
                    for q in range(2):
                        self.go(
                            s1.at[h, i, low(q)], u1.at[h, q], base + 20 * h + 16 + q,
                            self.place(h, 1 - 2 * q, 0),
                        )
                elif j != 0:
                    q = 0 if j == 1 else 1
                    self.got(u1.at[h, q], base + 20 * h + 16 + q)
                    s1[h, i] = total.astype(BF)
                    s1[h, i, low(q)] = (
                        total[16 * q : 16 * q + 16] + u1[h, q].astype(F32)
                    ).astype(BF)
                    self.go(
                        s1.at[h, i], u2.at[h, q], base + 20 * h + 18 + q, self.place(h, j, 0)
                    )
                else:
                    result[h] = total
        for h in range(2):
            for q in range(2):
                self.got(u2.at[h, q], base + 20 * h + 18 + q)
                result[h] = result[h] + u2[h, q].astype(F32)
        return jnp.concatenate(result, axis=0)


def merge_kernel(
    d_hbm, b_ref, order, out,
    d, ag, y, t1, t2, s1, u1, u2, gx, gy,
    lall, fall, swp, raw, rall, gram, glp, grp, grs, blk, zst,
    chain, half, left, right, scaled,
    dsem, ssem, rsem, cs, cr, ssem2, rsem2,
):
    plane = Plane(ssem, rsem)
    me = r = plane.r
    c = lax.axis_index("ckpt")
    side = lax.rem(c, 2)
    even = side == 0
    other = c + 1 - 2 * side
    load = pltpu.make_async_copy(d_hbm, d, dsem.at[0])
    load.start()
    barrier = pltpu.get_barrier_semaphore()

    @pl.loop(1, N)
    def _(k):
        pl.semaphore_signal(barrier, inc=1, device_id={"rows": lax.rem(r + k, N)}, device_id_type=MESH)
        pl.semaphore_signal(barrier, inc=1, device_id={"ckpt": lax.rem(c + k, N)}, device_id_type=MESH)

    ag[0, me] = b_ref[...]
    pl.semaphore_wait(barrier, 2 * N - 2)

    def columns(j):
        return pl.ds(pl.multiple_of(j * COLS, 128), COLS)

    def left_product(sweep, base):
        total = [jnp.zeros((RANK, ROWS), F32)]

        def ready(sources):
            for dx, dy in sources:
                source = plane.place(0, dx, dy)
                if (dx, dy) == (0, 0) and sweep == 0:
                    load.wait()
                total[0] = total[0] + dot_nt(ag[sweep, source], d[:, columns(source)])

        plane.gather(
            lambda h, o: ag.at[sweep, o, pl.ds(32 * h, 32)],
            lambda h, o, q: ag.at[sweep, o, pl.ds(32 * h + 16 * q, 16)],
            base,
            ready,
        )
        return total[0]

    def right_product(left16, sweep, base, label):
        return plane.scatter(
            lambda j: jnp.dot(left16, d[:, columns(label(j))], preferred_element_type=F32),
            *(ref.at[sweep] for ref in (y, t1, t2, s1, u1, u2)),
            base,
        )

    def exchange(buffer, axis, base):
        mine = plane.spot(axis, 0)
        for k in range(1, 4):
            plane.go(buffer.at[mine], buffer.at[mine], base + k, plane.place(axis, k, 0))

    def collect(buffer, axis, base):
        for k in range(1, 4):
            plane.got(buffer.at[plane.spot(axis, -k)], base + k)
        return (buffer[0] + buffer[1]) + (buffer[2] + buffer[3])

    facts = {}

    def gram_start(value, index):
        wide = dot_nt(value, jnp.concatenate([jnp.zeros_like(value), value], axis=0), HIGHEST)
        gx[index, plane.x] = pltpu.roll(wide[:32], RANK, 1) + wide[32:]
        exchange(gx.at[index], 0, 160 + 8 * index)

        def middle():
            gy[index, plane.y] = collect(gx.at[index], 0, 160 + 8 * index)
            exchange(gy.at[index], 1, 164 + 8 * index)

        def begin():
            total = collect(gy.at[index], 1, 164 + 8 * index)
            on_right = lax.broadcasted_iota(jnp.int32, (32, 128), 1) >= RANK
            upper = jnp.where(on_right, pltpu.roll(total, RANK, 1), 0.0)
            lower = jnp.where(on_right, total, 0.0)
            work = factor_start(jnp.concatenate([upper, lower], axis=0))
            facts[index] = factor_steps(work, 0, 16)

        def go_on(first):
            facts[index] = factor_steps(facts[index], first, first + 16)
            if first == 48:
                facts[index] = factor_end(facts[index])

        plane.tasks = [middle, begin] + [functools.partial(go_on, first) for first in (16, 32, 48)]

    def apply_inverse(index, value):
        return jnp.dot(facts[index][:, :RANK], value, precision=HIGHEST)

    left_raw = left_product(0, 0)
    gram_start(left_raw, 0)
    right_sum = right_product(left_raw.astype(BF), 0, 80, lambda j: j)
    right_raw = apply_inverse(0, right_sum)
    ag[1, me] = right_raw.astype(BF)
    gram_start(right_raw, 1)
    left_raw = apply_inverse(1, left_product(1, 40))
    gram_start(left_raw, 2)
    right_raw = apply_inverse(2, right_product(left_raw.astype(BF), 1, 120, lambda j: xor(j, c)))

    def rows64(i):
        return pl.ds(pl.multiple_of(i * RANK, RANK), RANK)

    def rows32(i):
        return pl.ds(pl.multiple_of(i * 32, 32), 32)

    def tile_of(i):
        return lax.rem(i, 2) * 512, pl.ds(pl.multiple_of(lax.div(i, 2) * 128, 128), 128)

    def send(axis, mine, src, dst, phase, k):
        return pltpu.make_async_remote_copy(
            src_ref=src,
            dst_ref=dst,
            send_sem=cs.at[phase, k],
            recv_sem=cr.at[phase, mine],
            device_id={axis: lax.rem(mine + k, N)},
            device_id_type=MESH,
        )

    def arrival(axis, buffer, phase, source):
        pltpu.make_async_remote_copy(
            src_ref=buffer,
            dst_ref=buffer,
            send_sem=cs.at[phase, 0],
            recv_sem=cr.at[phase, source],
            device_id={axis: source},
            device_id_type=MESH,
        ).wait_recv()

    def swap(h):
        return pltpu.make_async_remote_copy(
            src_ref=swp.at[pl.ds(32 * h, 32)],
            dst_ref=raw.at[r, pl.ds(32 * h, 32)],
            send_sem=cs.at[5, h],
            recv_sem=cr.at[5, h],
            device_id={"ckpt": xor(r, c)},
            device_id_type=MESH,
        )

    right16 = right_raw.astype(BF)

    @pl.when(r == 0)
    def _():
        raw[0] = right16

    @pl.when(r != 0)
    def _():
        swp[...] = right16
        swap(0).start()
        swap(1).start()

    gram_start(right_raw, 3)
    lall[rows64(c)] = apply_inverse(2, left_raw).astype(BF)

    @pl.loop(1, N)
    def _(k):
        send("ckpt", c, lall.at[rows64(c)], lall.at[rows64(c)], 0, k).start()

    plane.tick()

    def finish_fact():
        fall[rows64(c)] = facts[3].astype(BF)

        @pl.loop(1, N)
        def _(k):
            send("ckpt", c, fall.at[rows64(c)], fall.at[rows64(c)], 1, k).start()

    def left_gram():
        @pl.loop(1, N)
        def _(k):
            source = lax.rem(c + N - k, N)
            arrival("ckpt", lall.at[rows64(source)], 0, source)

        for part in range(2):
            strip = lall[pl.ds(pl.multiple_of(part * 512 + c * 32, 32), 32), :]
            product = dot_nt(strip, lall[...]).astype(BF)
            for q in range(8):
                glp[2 * q + part] = product[:, q * 128 : (q + 1) * 128]

        @pl.loop(1, N)
        def _(k):
            send("rows", r, glp.at[lax.rem(r + k, N)], grs.at[0, r], 2, k).start()

    plane.tasks = plane.tasks + [finish_fact, left_gram]

    def landed(h):
        @pl.when(r != 0)
        def _():
            swap(h).wait_recv()

    plane.gather(
        lambda h, o: raw.at[o, pl.ds(32 * h, 32)],
        lambda h, o, q: raw.at[o, pl.ds(32 * h + 16 * q, 16)],
        192,
        lambda sources: None,
        landed,
    )

    @pl.loop(1, N)
    def _(k):
        source = lax.rem(c + N - k, N)
        arrival("ckpt", fall.at[rows64(source)], 1, source)

    @pl.loop(0, N)
    def _(o):
        e = xor(o, c)
        rall[rows64(e), :] = jnp.dot(
            fall[rows64(e), :RANK], raw[o], preferred_element_type=F32
        ).astype(BF)

    first_row, pair = tile_of(r)
    pair_rows = pl.ds(pl.multiple_of(lax.div(r, 2) * 128, 128), 128)
    half_rows = pl.ds(pl.multiple_of(first_row, 512), 512)
    grp[...] = dot_nt(rall[half_rows, :], rall[pair_rows, :]).astype(BF)

    @pl.loop(1, N)
    def _(k):
        send("ckpt", c, grp.at[rows32(lax.rem(c + k, N))], grs.at[1, c], 3, k).start()

    def total_of(axis, mine, which, phase, first):
        def step(k, value):
            source = lax.rem(mine + N - k, N)
            arrival(axis, grs.at[which, source], phase, source)
            return value + grs[which, source].astype(F32)

        return lax.fori_loop(1, N, step, first.astype(F32)).astype(BF)

    blk[0] = total_of("rows", r, 0, 2, glp[r])
    blk[1] = total_of("ckpt", c, 1, 3, grp[rows32(c)])

    @pl.loop(1, N)
    def _(k):
        send("ckpt", c, blk.at[lax.rem(c + k, 2)], zst.at[rows32(c)], 4, k).start()

    zst[rows32(c)] = blk[side]

    @pl.loop(1, N)
    def _(k):
        source = lax.rem(c + N - k, N)
        arrival("ckpt", zst.at[rows32(source)], 4, source)

    gram[half_rows, pair] = zst[...]

    def gram_part(o, start, size):
        row, lanes = tile_of(o)
        return gram.at[pl.ds(pl.multiple_of(row + start, 128), size), lanes]

    plane.gather(
        lambda h, o: gram_part(o, 256 * h, 256),
        lambda h, o, q: gram_part(o, 256 * h + 128 * q, 128),
        232,
        lambda sources: None,
    )

    def to_other(src, dst, sem):
        return pltpu.make_async_remote_copy(
            src_ref=src,
            dst_ref=dst,
            send_sem=ssem2.at[sem],
            recv_sem=rsem2.at[sem],
            device_id={"ckpt": other},
            device_id_type=MESH,
        )

    @pl.when(~even)
    def _():
        to_other(gram, chain.at[1, 0], 0).start()

    def factors(step):
        return (1.5 / 4.0, -0.5 / 64.0) if step == 0 else (1.5, -0.5)

    def advance(dst, old, weights, lead, tail, tile):
        @pl.loop(0, ALL // tile)
        def _(i):
            part = pl.ds(pl.multiple_of(i * tile, tile), tile)
            product = jnp.dot(old[part, :], weights[...], preferred_element_type=F32)
            dst[part, :] = (lead * old[part, :].astype(F32) + tail * product).astype(BF)

    def apply(dst, old, grams, lead, tail, tile):
        @pl.loop(0, ALL // tile)
        def _(i):
            part = pl.ds(pl.multiple_of(i * tile, tile), tile)
            product = jnp.dot(grams[part, :], old[...], preferred_element_type=F32)
            dst[part, :] = (lead * old[part, :].astype(F32) + tail * product).astype(BF)

    for step in range(NS_ITERS - 1):
        current = gram if step == 0 else chain.at[side, step]
        advance(half, current, current, *factors(step), TILE)
        advance(chain.at[side, step + 1], half, current, *factors(step), TILE)

        @pl.when(~even)
        def _():
            to_other(chain.at[1, step + 1], chain.at[1, step + 1], step + 1).start()

    @pl.when(even)
    def _():
        for step in range(NS_ITERS):
            old = lall if step == 0 else left.at[(step - 1) % 2]
            current = gram if step == 0 else chain.at[0, step]
            apply(left.at[step % 2], old, current, *factors(step), TILE)
        for k in range(N):
            block = pl.ds(k * RANK, RANK)
            weight = (1 + order[k]).astype(F32) / N
            white = left[(NS_ITERS - 1) % 2, block, :]
            white = jnp.concatenate([jnp.zeros_like(white), white], axis=0)
            scaled[block, :] = (
                weight * jnp.dot(fall[block, :], white, preferred_element_type=F32)
            ).astype(BF)
        to_other(scaled, scaled, 4).start()
        for step in range(NS_ITERS):
            to_other(chain.at[1, step], chain.at[1, step], step).wait_recv()
            old = rall if step == 0 else right.at[(step - 1) % 2]
            apply(right.at[step % 2], old, chain.at[1, step], *factors(step), TILE)
        to_other(scaled, scaled, 4).wait_send()

    @pl.when(~even)
    def _():
        for step in range(NS_ITERS):
            old = rall if step == 0 else right.at[(step - 1) % 2]
            current = gram if step == 0 else chain.at[1, step]
            apply(right.at[step % 2], old, current, *factors(step), TILE)
        for step in range(NS_ITERS):
            to_other(chain.at[1, step], chain.at[1, step], step).wait_send()
        to_other(scaled, scaled, 4).wait_recv()

    out[...] = lax.dot_general(
        scaled[...], right[(NS_ITERS - 1) % 2], (((0,), (0,)), ((), ())), preferred_element_type=F32
    ).astype(BF)

    @pl.when(r != 0)
    def _():
        swap(0).wait_send()
        swap(1).wait_send()

    @pl.loop(1, N)
    def _(k):
        send("ckpt", c, lall.at[rows64(c)], lall.at[rows64(c)], 0, k).wait_send()
        send("ckpt", c, fall.at[rows64(c)], fall.at[rows64(c)], 1, k).wait_send()
        send("rows", r, glp.at[0], grs.at[0, r], 2, k).wait_send()
        send("ckpt", c, grp.at[rows32(c)], grs.at[1, c], 3, k).wait_send()
        send("ckpt", c, blk.at[0], zst.at[rows32(c)], 4, k).wait_send()

    plane.finish()


def body(deltas, start_basis, edit_order):
    vmem = pl.BlockSpec(memory_space=pltpu.VMEM)
    return pl.pallas_call(
        merge_kernel,
        out_shape=jax.ShapeDtypeStruct((ROWS, COLS), BF),
        in_specs=[
            pl.BlockSpec(memory_space=pl.ANY), vmem, pl.BlockSpec(memory_space=pltpu.SMEM),
        ],
        out_specs=vmem,
        scratch_shapes=[
            pltpu.VMEM((ROWS, N * COLS), BF),
            pltpu.VMEM((2, N, RANK, COLS), BF),
            pltpu.VMEM((2, 2, 4, 4, 32, COLS), BF),
            pltpu.VMEM((2, 2, 2, 4, 16, COLS), BF),
            pltpu.VMEM((2, 2, 2, 4, 32, COLS), BF),
            pltpu.VMEM((2, 2, 4, 32, COLS), BF),
            pltpu.VMEM((2, 2, 2, 16, COLS), BF),
            pltpu.VMEM((2, 2, 2, 32, COLS), BF),
            pltpu.VMEM((4, 4, 32, 128), F32),
            pltpu.VMEM((4, 4, 32, 128), F32),
            pltpu.VMEM((ALL, ROWS), BF),
            pltpu.VMEM((ALL, 2 * RANK), BF),
            pltpu.VMEM((RANK, COLS), BF),
            pltpu.VMEM((N, RANK, COLS), BF),
            pltpu.VMEM((ALL, COLS), BF),
            pltpu.VMEM((ALL, ALL), BF),
            pltpu.VMEM((N, 32, 128), BF),
            pltpu.VMEM((512, 128), BF),
            pltpu.VMEM((2, N, 32, 128), BF),
            pltpu.VMEM((2, 32, 128), BF),
            pltpu.VMEM((512, 128), BF),
            pltpu.VMEM((2, NS_ITERS, ALL, ALL), BF),
            pltpu.VMEM((ALL, ALL), BF),
            pltpu.VMEM((2, ALL, ROWS), BF),
            pltpu.VMEM((2, ALL, COLS), BF),
            pltpu.VMEM((ALL, ROWS), BF),
            pltpu.SemaphoreType.DMA((1,)),
            pltpu.SemaphoreType.DMA((272,)),
            pltpu.SemaphoreType.DMA((272,)),
            pltpu.SemaphoreType.DMA((6, N)),
            pltpu.SemaphoreType.DMA((6, N)),
            pltpu.SemaphoreType.DMA((5,)),
            pltpu.SemaphoreType.DMA((5,)),
        ],
        compiler_params=pltpu.CompilerParams(
            collective_id=0, has_side_effects=True, vmem_limit_bytes=55 * 1024 * 1024
        ),
        name="merge",
    )(deltas[0], start_basis[0].T, edit_order)


def solution(mesh):
    return jax.shard_map(
        body,
        mesh=mesh,
        in_specs=(P("ckpt", "rows", None), P("ckpt", "rows", None), P()),
        out_specs=P("rows", "ckpt"),
        check_vma=False,
    )
```

```python
import functools

import jax
import jax.numpy as jnp
from jax import lax
from jax.experimental import pallas as pl
from jax.experimental.pallas import tpu as pltpu
from jax.sharding import PartitionSpec as P

RANK = 64
NS_ITERS = 4
N = 16
COLS = 896
ROWS = 256
PACK = ROWS + 2 * RANK
ALL = N * RANK
TILE = 512
PIVOTS = 4
BF = jnp.bfloat16
F32 = jnp.float32
MESH = pl.DeviceIdType.MESH
HIGHEST = lax.Precision.HIGHEST
NT = (((1,), (1,)), ((), ()))


def dot_nt(a, b, precision=None):
    return lax.dot_general(a, b, NT, precision=precision, preferred_element_type=F32)


def factor_start(gram_wide):
    row = lax.broadcasted_iota(jnp.int32, (RANK, 2 * RANK), 0)
    lane = lax.broadcasted_iota(jnp.int32, (RANK, 2 * RANK), 1)
    return gram_wide + jnp.where(row == lane, 1.0, 0.0)


def factor_steps(work, first, last):
    row = lax.broadcasted_iota(jnp.int32, (RANK, 2 * RANK), 0)
    lane = lax.broadcasted_iota(jnp.int32, (RANK, 2 * RANK), 1)

    def step(i, w):
        p = [PIVOTS * i + k for k in range(PIVOTS)]
        rows = [jnp.sum(jnp.where(row == p[k], w, 0.0), axis=0, keepdims=True) for k in range(PIVOTS)]
        cols = [
            jnp.sum(jnp.where(lane == p[k] + RANK, w, 0.0), axis=1, keepdims=True)
            for k in range(PIVOTS)
        ]
        block = {
            (k, m): jnp.sum(jnp.where(lane[:1] == p[m] + RANK, rows[k], 0.0), axis=1, keepdims=True)
            for k in range(PIVOTS)
            for m in range(k, PIVOTS)
        }
        inverse = []
        for k in range(PIVOTS):
            inverse.append(1.0 / block[k, k])
            for n in range(k + 1, PIVOTS):
                ratio = block[k, n] * inverse[k]
                rows[n] = rows[n] - ratio * rows[k]
                for m in range(n, PIVOTS):
                    block[n, m] = block[n, m] - ratio * block[k, m]
        for k in range(PIVOTS):
            ratio = jnp.where(row[:, :1] > p[k], cols[k], 0.0) * inverse[k]
            for m in range(k + 1, PIVOTS):
                cols[m] = cols[m] - ratio * block[k, m]
            w = w - ratio * rows[k]
        return w

    return lax.fori_loop(first // PIVOTS, last // PIVOTS, step, work)


def factor_end(work):
    row = lax.broadcasted_iota(jnp.int32, (RANK, 2 * RANK), 0)
    lane = lax.broadcasted_iota(jnp.int32, (RANK, 2 * RANK), 1)
    diagonal = jnp.sum(jnp.where(lane == row + RANK, work, 0.0), axis=1, keepdims=True)
    return work * lax.rsqrt(diagonal)


def xor(a, b):
    return sum(bit * lax.rem(lax.div(a, bit) + lax.div(b, bit), 2) for bit in (1, 2, 4, 8))


OFFSETS = (0, -1, 1, 2)
FAR_FIRST = (2, 1, -1, 0)


class Plane:
    def __init__(self, ssem, rsem):
        self.ssem, self.rsem = ssem, rsem
        self.r = lax.axis_index("rows")
        self.x, self.y = lax.rem(self.r, 4), lax.div(self.r, 4)
        self.sends = []
        self.tasks = []

    def place(self, axis, da, db):
        dx, dy = (da, db) if axis == 0 else (db, da)
        return lax.rem(self.y + dy + 4, 4) * 4 + lax.rem(self.x + dx + 4, 4)

    def spot(self, axis, delta):
        return lax.rem((self.x if axis == 0 else self.y) + delta + 4, 4)

    def copy(self, src, dst, sem, to):
        return pltpu.make_async_remote_copy(
            src_ref=src,
            dst_ref=dst,
            send_sem=self.ssem.at[sem],
            recv_sem=self.rsem.at[sem],
            device_id={"rows": to},
            device_id_type=MESH,
        )

    def go(self, src, dst, sem, to):
        copy = self.copy(src, dst, sem, to)
        copy.start()
        self.sends.append(copy)

    def got(self, dst, sem):
        self.copy(dst, dst, sem, self.r).wait_recv()

    def tick(self):
        if self.tasks:
            self.tasks.pop(0)()

    def flush(self):
        while self.tasks:
            self.tick()

    def finish(self):
        for copy in self.sends:
            copy.wait_send()

    def gather(self, half, quarter, base, ready, landed=None):
        def send(ref, h, slot, da, db):
            self.go(ref, ref, base + 20 * h + slot, self.place(h, da, db))

        def take(ref, h, slot):
            self.got(ref, base + 20 * h + slot)

        def spread(h, j):
            origin = self.place(h, OFFSETS[j], 0)
            send(half(h, origin), h, 4 + j, 0, 1)
            send(half(h, origin), h, 8 + j, 0, -1)

        def relay(h, j):
            origin = self.place(h, OFFSETS[j], -1)
            take(half(h, origin), h, 4 + j)
            send(quarter(h, origin, 0), h, 12 + j, 0, 1)
            origin = self.place(h, OFFSETS[j], 1)
            take(half(h, origin), h, 8 + j)
            send(quarter(h, origin, 1), h, 16 + j, 0, -1)

        for h in range(2):
            if landed is not None:
                landed(h)
            send(half(h, self.r), h, 0, 1, 0)
            send(half(h, self.r), h, 1, -1, 0)
            spread(h, 0)
        ready([(0, 0)])
        self.tick()
        for h in range(2):
            origin = self.place(h, -1, 0)
            take(half(h, origin), h, 0)
            send(quarter(h, origin, 0), h, 2, 1, 0)
            origin = self.place(h, 1, 0)
            take(half(h, origin), h, 1)
            send(quarter(h, origin, 1), h, 3, -1, 0)
        for h in range(2):
            spread(h, 1)
            spread(h, 2)
        self.tick()
        for h in range(2):
            relay(h, 0)
        for h in range(2):
            origin = self.place(h, 2, 0)
            take(quarter(h, origin, 0), h, 2)
            take(quarter(h, origin, 1), h, 3)
            spread(h, 3)
        ready([(-1, 0), (1, 0), (0, -1), (0, 1)])
        self.tick()
        for j in (1, 2):
            for h in range(2):
                relay(h, j)
        self.tick()
        ready([(-1, -1), (1, -1), (-1, 1), (1, 1)])
        for h in range(2):
            relay(h, 3)
        self.tick()
        groups = ([(0, 2), (2, 0)], [(-1, 2), (2, -1)], [(1, 2), (2, 1)], [(2, 2)])
        for j in range(4):
            for h in range(2):
                origin = self.place(h, OFFSETS[j], 2)
                take(quarter(h, origin, 0), h, 12 + j)
                take(quarter(h, origin, 1), h, 16 + j)
            ready(groups[j])
        self.flush()

    def scatter(self, part, y, t1, t2, s1, u1, u2, base):
        done = set()

        def make(dx, dy):
            if (dx, dy) in done:
                return
            done.add((dx, dy))
            xs, ys = self.spot(0, dx), self.spot(1, dy)
            value = part(ys * 4 + xs).astype(BF)
            y[0, ys, xs] = value[:32]
            y[1, xs, ys] = value[32:]

        def low(q):
            return pl.ds(16 * q, 16)

        for i, j in enumerate(FAR_FIRST):
            for h in range(2):
                make(*((j, 2) if h == 0 else (2, j)))
                b, a = self.spot(1 - h, 2), self.spot(h, j)
                for q in range(2):
                    self.go(
                        y.at[h, b, a, low(q)], t1.at[h, q, i], base + 20 * h + 4 * q + i,
                        self.place(h, 0, 1 - 2 * q),
                    )
        self.tick()
        for i, j in enumerate(FAR_FIRST):
            for h in range(2):
                for q in range(2):
                    delta = 1 - 2 * q
                    make(*((j, delta) if h == 0 else (delta, j)))
                    b, a = self.spot(1 - h, delta), self.spot(h, j)
                    self.got(t1.at[h, q, i], base + 20 * h + 4 * q + i)
                    y[h, b, a, low(q)] = (
                        y[h, b, a, low(q)].astype(F32) + t1[h, q, i].astype(F32)
                    ).astype(BF)
                    self.go(
                        y.at[h, b, a], t2.at[h, q, i], base + 20 * h + 8 + 4 * q + i,
                        self.place(h, 0, delta),
                    )
            self.tick()
        make(0, 0)
        self.flush()
        result = [None, None]
        for i, j in enumerate(FAR_FIRST):
            for h in range(2):
                b, a = self.spot(1 - h, 0), self.spot(h, j)
                make(*((j, 0) if h == 0 else (0, j)))
                self.got(t2.at[h, 0, i], base + 20 * h + 8 + i)
                self.got(t2.at[h, 1, i], base + 20 * h + 12 + i)
                total = y[h, b, a].astype(F32) + t2[h, 0, i].astype(F32) + t2[h, 1, i].astype(F32)
                if j == 2:
                    s1[h, i] = total.astype(BF)
                    for q in range(2):
                        self.go(
                            s1.at[h, i, low(q)], u1.at[h, q], base + 20 * h + 16 + q,
                            self.place(h, 1 - 2 * q, 0),
                        )
                elif j != 0:
                    q = 0 if j == 1 else 1
                    self.got(u1.at[h, q], base + 20 * h + 16 + q)
                    s1[h, i] = total.astype(BF)
                    s1[h, i, low(q)] = (
                        total[16 * q : 16 * q + 16] + u1[h, q].astype(F32)
                    ).astype(BF)
                    self.go(
                        s1.at[h, i], u2.at[h, q], base + 20 * h + 18 + q, self.place(h, j, 0)
                    )
                else:
                    result[h] = total
        for h in range(2):
            for q in range(2):
                self.got(u2.at[h, q], base + 20 * h + 18 + q)
                result[h] = result[h] + u2[h, q].astype(F32)
        return jnp.concatenate(result, axis=0)


def merge_kernel(
    d_hbm, b_ref, order, out,
    d, ag, y, t1, t2, s1, u1, u2, gx, gy,
    lall, fall, swp, raw, rall, gram, glp, grp, grs, blk, zst,
    chain, half, left, right, scaled,
    dsem, ssem, rsem, cs, cr, ssem2, rsem2,
):
    plane = Plane(ssem, rsem)
    me = r = plane.r
    c = lax.axis_index("ckpt")
    side = lax.rem(c, 2)
    even = side == 0
    other = c + 1 - 2 * side
    load = pltpu.make_async_copy(d_hbm, d, dsem.at[0])
    load.start()
    barrier = pltpu.get_barrier_semaphore()

    @pl.loop(1, N)
    def _(k):
        pl.semaphore_signal(barrier, inc=1, device_id={"rows": lax.rem(r + k, N)}, device_id_type=MESH)
        pl.semaphore_signal(barrier, inc=1, device_id={"ckpt": lax.rem(c + k, N)}, device_id_type=MESH)

    ag[0, me] = b_ref[...]
    pl.semaphore_wait(barrier, 2 * N - 2)

    def columns(j):
        return pl.ds(pl.multiple_of(j * COLS, 128), COLS)

    def left_product(sweep, base):
        total = [jnp.zeros((RANK, ROWS), F32)]

        def ready(sources):
            for dx, dy in sources:
                source = plane.place(0, dx, dy)
                if (dx, dy) == (0, 0) and sweep == 0:
                    load.wait()
                total[0] = total[0] + dot_nt(ag[sweep, source], d[:, columns(source)])

        plane.gather(
            lambda h, o: ag.at[sweep, o, pl.ds(32 * h, 32)],
            lambda h, o, q: ag.at[sweep, o, pl.ds(32 * h + 16 * q, 16)],
            base,
            ready,
        )
        return total[0]

    def right_product(left16, sweep, base, label):
        return plane.scatter(
            lambda j: jnp.dot(left16, d[:, columns(label(j))], preferred_element_type=F32),
            *(ref.at[sweep] for ref in (y, t1, t2, s1, u1, u2)),
            base,
        )

    def exchange(buffer, axis, base):
        mine = plane.spot(axis, 0)
        for k in range(1, 4):
            plane.go(buffer.at[mine], buffer.at[mine], base + k, plane.place(axis, k, 0))

    def collect(buffer, axis, base):
        for k in range(1, 4):
            plane.got(buffer.at[plane.spot(axis, -k)], base + k)
        return (buffer[0] + buffer[1]) + (buffer[2] + buffer[3])

    facts = {}

    def gram_start(value, index):
        wide = dot_nt(value, jnp.concatenate([jnp.zeros_like(value), value], axis=0), HIGHEST)
        gx[index, plane.x] = pltpu.roll(wide[:32], RANK, 1) + wide[32:]
        exchange(gx.at[index], 0, 160 + 8 * index)

        def middle():
            gy[index, plane.y] = collect(gx.at[index], 0, 160 + 8 * index)
            exchange(gy.at[index], 1, 164 + 8 * index)

        def begin():
            total = collect(gy.at[index], 1, 164 + 8 * index)
            on_right = lax.broadcasted_iota(jnp.int32, (32, 128), 1) >= RANK
            upper = jnp.where(on_right, pltpu.roll(total, RANK, 1), 0.0)
            lower = jnp.where(on_right, total, 0.0)
            work = factor_start(jnp.concatenate([upper, lower], axis=0))
            facts[index] = factor_steps(work, 0, 16)

        def go_on(first):
            facts[index] = factor_steps(facts[index], first, first + 16)
            if first == 48:
                facts[index] = factor_end(facts[index])

        plane.tasks = [middle, begin] + [functools.partial(go_on, first) for first in (16, 32, 48)]

    def apply_inverse(index, value):
        return jnp.dot(facts[index][:, :RANK], value, precision=HIGHEST)

    left_raw = left_product(0, 0)
    gram_start(left_raw, 0)
    right_sum = right_product(left_raw.astype(BF), 0, 80, lambda j: j)
    right_raw = apply_inverse(0, right_sum)
    ag[1, me] = right_raw.astype(BF)
    gram_start(right_raw, 1)
    left_raw = apply_inverse(1, left_product(1, 40))
    gram_start(left_raw, 2)
    right_raw = apply_inverse(2, right_product(left_raw.astype(BF), 1, 120, lambda j: xor(j, c)))

    def rows64(i):
        return pl.ds(pl.multiple_of(i * RANK, RANK), RANK)

    def rows32(i):
        return pl.ds(pl.multiple_of(i * 32, 32), 32)

    def tile_of(i):
        return lax.rem(i, 2) * 512, pl.ds(pl.multiple_of(lax.div(i, 2) * 128, 128), 128)

    def send(axis, mine, src, dst, phase, k):
        return pltpu.make_async_remote_copy(
            src_ref=src,
            dst_ref=dst,
            send_sem=cs.at[phase, k],
            recv_sem=cr.at[phase, mine],
            device_id={axis: lax.rem(mine + k, N)},
            device_id_type=MESH,
        )

    def arrival(axis, buffer, phase, source):
        pltpu.make_async_remote_copy(
            src_ref=buffer,
            dst_ref=buffer,
            send_sem=cs.at[phase, 0],
            recv_sem=cr.at[phase, source],
            device_id={axis: source},
            device_id_type=MESH,
        ).wait_recv()

    def swap(h):
        return pltpu.make_async_remote_copy(
            src_ref=swp.at[pl.ds(32 * h, 32)],
            dst_ref=raw.at[r, pl.ds(32 * h, 32)],
            send_sem=cs.at[5, h],
            recv_sem=cr.at[5, h],
            device_id={"ckpt": xor(r, c)},
            device_id_type=MESH,
        )

    right16 = right_raw.astype(BF)

    @pl.when(r == 0)
    def _():
        raw[0] = right16

    @pl.when(r != 0)
    def _():
        swp[...] = right16
        swap(0).start()
        swap(1).start()

    gram_start(right_raw, 3)
    lall[rows64(c)] = apply_inverse(2, left_raw).astype(BF)

    @pl.loop(1, N)
    def _(k):
        send("ckpt", c, lall.at[rows64(c)], lall.at[rows64(c)], 0, k).start()

    plane.tick()

    def finish_fact():
        fall[rows64(c)] = facts[3].astype(BF)

        @pl.loop(1, N)
        def _(k):
            send("ckpt", c, fall.at[rows64(c)], fall.at[rows64(c)], 1, k).start()

    def left_gram():
        @pl.loop(1, N)
        def _(k):
            source = lax.rem(c + N - k, N)
            arrival("ckpt", lall.at[rows64(source)], 0, source)

        for part in range(2):
            strip = lall[pl.ds(pl.multiple_of(part * 512 + c * 32, 32), 32), :]
            product = dot_nt(strip, lall[...]).astype(BF)
            for q in range(8):
                glp[2 * q + part] = product[:, q * 128 : (q + 1) * 128]

        @pl.loop(1, N)
        def _(k):
            send("rows", r, glp.at[lax.rem(r + k, N)], grs.at[0, r], 2, k).start()

    plane.tasks = plane.tasks + [finish_fact, left_gram]
    plane.tick()
    plane.tick()
    pending, groups = [], []

    def solve(sources):
        pending.extend(sources)
        groups.append(len(sources))
        if len(groups) < 4:
            return
        if len(groups) == 4:

            @pl.loop(1, N)
            def _(k):
                source = lax.rem(c + N - k, N)
                arrival("ckpt", fall.at[rows64(source)], 1, source)

        for dx, dy in pending:
            o = plane.place(0, dx, dy)
            block = rows64(xor(o, c))
            rall[block, :] = jnp.dot(
                fall[block, :RANK], raw[o], preferred_element_type=F32
            ).astype(BF)
        pending.clear()

    def landed(h):
        @pl.when(r != 0)
        def _():
            swap(h).wait_recv()

    plane.gather(
        lambda h, o: raw.at[o, pl.ds(32 * h, 32)],
        lambda h, o, q: raw.at[o, pl.ds(32 * h + 16 * q, 16)],
        192,
        solve,
        landed,
    )
    first_row, pair = tile_of(r)
    pair_rows = pl.ds(pl.multiple_of(lax.div(r, 2) * 128, 128), 128)
    half_rows = pl.ds(pl.multiple_of(first_row, 512), 512)
    grp[...] = dot_nt(rall[half_rows, :], rall[pair_rows, :]).astype(BF)

    @pl.loop(1, N)
    def _(k):
        send("ckpt", c, grp.at[rows32(lax.rem(c + k, N))], grs.at[1, c], 3, k).start()

    def total_of(axis, mine, which, phase, first):
        def step(k, value):
            source = lax.rem(mine + N - k, N)
            arrival(axis, grs.at[which, source], phase, source)
            return value + grs[which, source].astype(F32)

        return lax.fori_loop(1, N, step, first.astype(F32)).astype(BF)

    blk[0] = total_of("rows", r, 0, 2, glp[r])
    blk[1] = total_of("ckpt", c, 1, 3, grp[rows32(c)])

    @pl.loop(1, N)
    def _(k):
        send("ckpt", c, blk.at[lax.rem(c + k, 2)], zst.at[rows32(c)], 4, k).start()

    zst[rows32(c)] = blk[side]

    @pl.loop(1, N)
    def _(k):
        source = lax.rem(c + N - k, N)
        arrival("ckpt", zst.at[rows32(source)], 4, source)

    gram[half_rows, pair] = zst[...]

    def gram_part(o, start, size):
        row, lanes = tile_of(o)
        return gram.at[pl.ds(pl.multiple_of(row + start, 128), size), lanes]

    plane.gather(
        lambda h, o: gram_part(o, 256 * h, 256),
        lambda h, o, q: gram_part(o, 256 * h + 128 * q, 128),
        232,
        lambda sources: None,
    )

    def to_other(src, dst, sem):
        return pltpu.make_async_remote_copy(
            src_ref=src,
            dst_ref=dst,
            send_sem=ssem2.at[sem],
            recv_sem=rsem2.at[sem],
            device_id={"ckpt": other},
            device_id_type=MESH,
        )

    @pl.when(~even)
    def _():
        to_other(gram, chain.at[1, 0], 0).start()

    def factors(step):
        return (1.5 / 4.0, -0.5 / 64.0) if step == 0 else (1.5, -0.5)

    def advance(dst, old, weights, lead, tail, tile):
        @pl.loop(0, ALL // tile)
        def _(i):
            part = pl.ds(pl.multiple_of(i * tile, tile), tile)
            product = jnp.dot(old[part, :], weights[...], preferred_element_type=F32)
            dst[part, :] = (lead * old[part, :].astype(F32) + tail * product).astype(BF)

    def apply(dst, old, grams, lead, tail, tile):
        @pl.loop(0, ALL // tile)
        def _(i):
            part = pl.ds(pl.multiple_of(i * tile, tile), tile)
            product = jnp.dot(grams[part, :], old[...], preferred_element_type=F32)
            dst[part, :] = (lead * old[part, :].astype(F32) + tail * product).astype(BF)

    for step in range(NS_ITERS - 1):
        current = gram if step == 0 else chain.at[side, step]
        advance(half, current, current, *factors(step), TILE)
        advance(chain.at[side, step + 1], half, current, *factors(step), TILE)

        @pl.when(~even)
        def _():
            to_other(chain.at[1, step + 1], chain.at[1, step + 1], step + 1).start()

    @pl.when(even)
    def _():
        for step in range(NS_ITERS):
            old = lall if step == 0 else left.at[(step - 1) % 2]
            current = gram if step == 0 else chain.at[0, step]
            apply(left.at[step % 2], old, current, *factors(step), TILE)
        for k in range(N):
            block = pl.ds(k * RANK, RANK)
            weight = (1 + order[k]).astype(F32) / N
            white = left[(NS_ITERS - 1) % 2, block, :]
            white = jnp.concatenate([jnp.zeros_like(white), white], axis=0)
            scaled[block, :] = (
                weight * jnp.dot(fall[block, :], white, preferred_element_type=F32)
            ).astype(BF)
        to_other(scaled, scaled, 4).start()
        for step in range(NS_ITERS):
            to_other(chain.at[1, step], chain.at[1, step], step).wait_recv()
            old = rall if step == 0 else right.at[(step - 1) % 2]
            apply(right.at[step % 2], old, chain.at[1, step], *factors(step), TILE)
        to_other(scaled, scaled, 4).wait_send()

    @pl.when(~even)
    def _():
        for step in range(NS_ITERS):
            old = rall if step == 0 else right.at[(step - 1) % 2]
            current = gram if step == 0 else chain.at[1, step]
            apply(right.at[step % 2], old, current, *factors(step), TILE)
        for step in range(NS_ITERS):
            to_other(chain.at[1, step], chain.at[1, step], step).wait_send()
        to_other(scaled, scaled, 4).wait_recv()

    out[...] = lax.dot_general(
        scaled[...], right[(NS_ITERS - 1) % 2], (((0,), (0,)), ((), ())), preferred_element_type=F32
    ).astype(BF)

    @pl.when(r != 0)
    def _():
        swap(0).wait_send()
        swap(1).wait_send()

    @pl.loop(1, N)
    def _(k):
        send("ckpt", c, lall.at[rows64(c)], lall.at[rows64(c)], 0, k).wait_send()
        send("ckpt", c, fall.at[rows64(c)], fall.at[rows64(c)], 1, k).wait_send()
        send("rows", r, glp.at[0], grs.at[0, r], 2, k).wait_send()
        send("ckpt", c, grp.at[rows32(c)], grs.at[1, c], 3, k).wait_send()
        send("ckpt", c, blk.at[0], zst.at[rows32(c)], 4, k).wait_send()

    plane.finish()


def body(deltas, start_basis, edit_order):
    vmem = pl.BlockSpec(memory_space=pltpu.VMEM)
    return pl.pallas_call(
        merge_kernel,
        out_shape=jax.ShapeDtypeStruct((ROWS, COLS), BF),
        in_specs=[
            pl.BlockSpec(memory_space=pl.ANY), vmem, pl.BlockSpec(memory_space=pltpu.SMEM),
        ],
        out_specs=vmem,
        scratch_shapes=[
            pltpu.VMEM((ROWS, N * COLS), BF),
            pltpu.VMEM((2, N, RANK, COLS), BF),
            pltpu.VMEM((2, 2, 4, 4, 32, COLS), BF),
            pltpu.VMEM((2, 2, 2, 4, 16, COLS), BF),
            pltpu.VMEM((2, 2, 2, 4, 32, COLS), BF),
            pltpu.VMEM((2, 2, 4, 32, COLS), BF),
            pltpu.VMEM((2, 2, 2, 16, COLS), BF),
            pltpu.VMEM((2, 2, 2, 32, COLS), BF),
            pltpu.VMEM((4, 4, 32, 128), F32),
            pltpu.VMEM((4, 4, 32, 128), F32),
            pltpu.VMEM((ALL, ROWS), BF),
            pltpu.VMEM((ALL, 2 * RANK), BF),
            pltpu.VMEM((RANK, COLS), BF),
            pltpu.VMEM((N, RANK, COLS), BF),
            pltpu.VMEM((ALL, COLS), BF),
            pltpu.VMEM((ALL, ALL), BF),
            pltpu.VMEM((N, 32, 128), BF),
            pltpu.VMEM((512, 128), BF),
            pltpu.VMEM((2, N, 32, 128), BF),
            pltpu.VMEM((2, 32, 128), BF),
            pltpu.VMEM((512, 128), BF),
            pltpu.VMEM((2, NS_ITERS, ALL, ALL), BF),
            pltpu.VMEM((ALL, ALL), BF),
            pltpu.VMEM((2, ALL, ROWS), BF),
            pltpu.VMEM((2, ALL, COLS), BF),
            pltpu.VMEM((ALL, ROWS), BF),
            pltpu.SemaphoreType.DMA((1,)),
            pltpu.SemaphoreType.DMA((272,)),
            pltpu.SemaphoreType.DMA((272,)),
            pltpu.SemaphoreType.DMA((6, N)),
            pltpu.SemaphoreType.DMA((6, N)),
            pltpu.SemaphoreType.DMA((5,)),
            pltpu.SemaphoreType.DMA((5,)),
        ],
        compiler_params=pltpu.CompilerParams(
            collective_id=0, has_side_effects=True, vmem_limit_bytes=55 * 1024 * 1024
        ),
        name="merge",
    )(deltas[0], start_basis[0].T, edit_order)


def solution(mesh):
    return jax.shard_map(
        body,
        mesh=mesh,
        in_specs=(P("ckpt", "rows", None), P("ckpt", "rows", None), P()),
        out_specs=P("rows", "ckpt"),
        check_vma=False,
    )
```
